128 devices in a mesh: aux: 8 (over y, x_hi), pair: 16 (over x_lo, z, core).
Axes of the slice: x: 4 (x_hi: 2, x_lo: 2; x = x_hi * 2 + x_lo), y: 4, z: 4, core: 2. Of those that a mesh axis runs over, the one named last changes fastest.
Arguments:
- three_centre: bfloat16 [32, 128, 8, 64, 512], P('pair', 'aux'), may hold values from -6 to 6
- slot_groups: int32 [32, 128], P('pair', 'aux'), may hold values from 0 to 127, as said below
- slot_count: int32 [32, 8], P('pair', 'aux'), may hold values from 1 to 16, as said below
- block_cost: int32 [32, 128], P('pair', 'aux'), may hold values from 1 to 4
- green_occ: bfloat16 [32, 512, 128], P('pair'), may hold values from -0.25 to 0.25
- green_vir: bfloat16 [32, 64, 128], P('pair'), may hold values from -0.75 to 0.75
- target: bfloat16 [1024, 32, 128, 128], P(None, 'pair', 'aux'), may hold values from -0.0390625 to 0.0390625
Outputs:
- response: float32 [1024, 1024], P('aux', 'pair')
The draws below stay inside these ranges and needn't reach their ends.
Inputs may be any that keep to these rules, and one draw needn't show every extreme that they name: Each row of slot_groups is a permutation of 0 to 127. `slot_count`: in every orbital block some device has all its slots live.
All inputs are finite; a program needn't handle non-finite values.
Results may differ from the reference program's by a relative error of at most 0.0041.
Values may be sent and summed in bfloat16 or wider, within the bound.
No kernel may reach another device: no remote copies, remote signals or barrier semaphores. Data moves between devices by JAX's collectives and lax.ppermute only.
A program may use at most 128 MiB of HBM per device.

```python
import jax
import jax.numpy as jnp
from jax import lax

NAUX = 1024
AUXG = 8
MU = 512
NU = 64
LAM = 128
SIG = 128
MUC = 128
NGROUPS = 128
NBLK = 32
N_AUX = 8


def draw_slot_groups(key, part):
    subkeys = jax.random.split(key, NBLK)

    def shuffle(subkey):
        return jax.random.permutation(subkey, NGROUPS)
    return jax.vmap(shuffle)(subkeys).astype(jnp.int32)


def draw_slot_count(key, part):
    slots_each = NGROUPS // N_AUX
    key_one, key_two, key_three, key_four = jax.random.split(key, 4)
    shape = (NBLK, N_AUX)
    least = jnp.minimum(jax.random.randint(key_one, shape, 1, slots_each + 1), jax.random.randint(key_two, shape, 1, slots_each + 1))
    least = jnp.minimum(least, jax.random.randint(key_three, shape, 1, slots_each + 1))
    chosen = jax.random.randint(key_four, (NBLK, 1), 0, N_AUX)
    column = jnp.arange(N_AUX, dtype=jnp.int32)[None, :]
    return jnp.where(column == chosen, slots_each, least).astype(jnp.int32)


def plant(values, key, low, high):
    longest = values.shape.index(max(values.shape))
    spots = []
    for shift in (0, 1):
        where = [jax.random.randint(jax.random.fold_in(key, axis), (), 0, length) for axis, length in enumerate(values.shape)]
        where[longest] = (where[longest] + shift) % values.shape[longest]
        spots.append(tuple(where))
    return values.at[spots[0]].set(low).at[spots[1]].set(high)


def shard_levels(own_key, shape, shards, low, top_value):
    level, own = 1.0, jax.random.fold_in(own_key, 6)
    for dim, blocks in shards:
        draws = jnp.exp(jax.random.uniform(jax.random.fold_in(own, dim), (blocks,), jnp.float32, low / len(shards), top_value / len(shards)))
        level = level * jnp.repeat(draws, shape[dim] // blocks).reshape([-1 if axis == dim else 1 for axis in range(len(shape))])
    return level


def gaussian(own_key, extent, deviation, limit, pieces=(), held_as=jnp.bfloat16):
    result = deviation * jax.random.normal(own_key, extent, jnp.float32)
    if pieces:
        result = result * shard_levels(own_key, extent, pieces, -0.22, 0.18)
    return jnp.clip(result, -limit, limit).astype(held_as)


def setup_inputs(seed: int = 0) -> dict:
    streams_of = jax.random.split(jax.random.key(seed), 8)
    three_centre = gaussian(streams_of[0], (NBLK, NGROUPS, AUXG, NU, MU), 1.0, 6.0, ((0, 16), (1, 8)))
    slot_groups = draw_slot_groups(jax.random.fold_in(streams_of[7], 71), 0)
    slot_count = draw_slot_count(jax.random.fold_in(streams_of[7], 71), 0)
    block_cost = plant(jax.random.randint(streams_of[3], (NBLK, NGROUPS), 1, MU // MUC + 1), jax.random.fold_in(streams_of[3], 1), 1, (MU // MUC + 1) - 1).astype(jnp.int32)
    green_occ = gaussian(streams_of[4], (NBLK, MU, LAM), MU ** -0.5, 0.25, ((0, 16),))
    green_vir = gaussian(streams_of[5], (NBLK, NU, SIG), NU ** -0.5, 0.75, ((0, 16),))
    target = gaussian(streams_of[6], (NAUX, NBLK, LAM, SIG), (2.0 / (NBLK * LAM * SIG) ** 0.5), 0.0390625, ((1, 16), (2, 8)))
    return {"three_centre": three_centre, "slot_groups": slot_groups, "slot_count": slot_count, "block_cost": block_cost, "green_occ": green_occ, "green_vir": green_vir, "target": target}


def reference(three_centre, slot_groups, slot_count, block_cost, green_occ, green_vir, target):
    slots_each = NGROUPS // N_AUX
    position = jnp.arange(NGROUPS, dtype=jnp.int32)
    orbital = jnp.arange(MU, dtype=jnp.int32)

    def per_block(running, inputs):
        tensor, groups, counts, costs, occupied, virtual, columns = inputs
        live = (position % slots_each) < counts[position // slots_each]
        kept = orbital[None, :] < (MUC * costs)[:, None]
        masked = jnp.where(kept[:, None, None, :], tensor, jnp.zeros((), tensor.dtype))
        half = jnp.dot(masked.reshape(-1, MU), occupied, preferred_element_type=jnp.float32).astype(jnp.bfloat16)
        half = half.reshape(NGROUPS, AUXG, NU, LAM).transpose(0, 1, 3, 2).reshape(-1, NU)
        moved = jnp.dot(half, virtual, preferred_element_type=jnp.float32).astype(jnp.bfloat16)
        moved = moved.reshape(NGROUPS, AUXG * LAM * SIG)
        moved = jnp.where(live[:, None], moved, jnp.zeros((), moved.dtype))
        dense_rows = jnp.zeros_like(moved).at[groups].set(moved).reshape(NAUX, LAM * SIG)
        product = jnp.dot(dense_rows, columns.reshape(NAUX, LAM * SIG).T, preferred_element_type=jnp.float32)
        return running + product, None

    start_value = jnp.zeros((NAUX, NAUX), jnp.float32)
    inputs = (three_centre, slot_groups, slot_count, block_cost, green_occ, green_vir, jnp.moveaxis(target, 1, 0))
    response, _ = lax.scan(per_block, start_value, inputs)
    return response
```

```python
import jax
import jax.numpy as jnp
from jax import lax
from jax.experimental import pallas as pl
from jax.experimental.pallas import tpu as pltpu
from jax.sharding import PartitionSpec as P

NAUX = 1024
AUXG = 8
MU = 512
NU = 64
LAM = 128
SIG = 128
MUC = 128
NGROUPS = 128
DEPTH = 4
BF16 = jnp.bfloat16
F32 = jnp.float32


def half_kernel(count, cost, x_hbm, occ, header, o_ref, xbuf, sem):
    blocks, slots = x_hbm.shape[:2]
    dests = o_ref.shape[0]
    lam_each = LAM // dests
    units = MU // MUC
    for d in range(dests):
        o_ref[d, blocks * slots * lam_each:, :] = header[...]
    first = count[0]
    total = first + count[1]

    def place(i):
        b = jnp.where(i < first, 0, 1)
        return b, i - b * first

    def copy(i, k):
        b, s = place(i)
        slot = lax.rem(i, DEPTH)
        return pltpu.make_async_copy(
            x_hbm.at[b, s, :, :, pl.ds(0, MUC * k)],
            xbuf.at[slot, :, :, pl.ds(0, MUC * k)],
            sem.at[slot],
        )

    def cost_of(i):
        b, s = place(i)
        return cost[b * slots + s]

    def issue(i):
        c = cost_of(i)
        for k in range(1, units + 1):
            @pl.when(c == k)
            def _(k=k):
                copy(i, k).start()

    for i in range(DEPTH - 1):
        @pl.when(i < total)
        def _(i=i):
            issue(i)

    def step(i, carry):
        b, s = place(i)
        slot = lax.rem(i, DEPTH)

        @pl.when(i + DEPTH - 1 < total)
        def _():
            issue(i + DEPTH - 1)

        c = cost_of(i)
        for k in range(1, units + 1):
            @pl.when(c == k)
            def _(k=k):
                copy(i, k).wait()
                x = xbuf[slot, :, :, 0:MUC * k].reshape(AUXG * NU, MUC * k)
                h = jnp.dot(x, occ[b, 0:MUC * k, :], preferred_element_type=F32)
                ht = h.T.astype(BF16)
                row = pl.multiple_of((b * slots + s) * lam_each, lam_each)
                for d in range(dests):
                    o_ref[d, pl.ds(row, lam_each), :] = ht[d * lam_each:(d + 1) * lam_each]
        return carry

    lax.fori_loop(0, total, step, 0)


ROWS = NAUX + 32


def response_kernel(count, label, core, h_hbm, wide_vir, t_hbm, keep_ref, send_ref,
                    hbuf, tbuf, z, lhs, acc, r, order, hsem, tsem):
    sources = h_hbm.shape[0]
    blocks = wide_vir.shape[0]
    lam_each = LAM // sources
    slots = NGROUPS // sources
    depth = lam_each * SIG
    rows_h = blocks * slots * lam_each

    def h_copy(s):
        return pltpu.make_async_copy(h_hbm.at[s, pl.ds(0, rows_h), :], hbuf.at[s], hsem.at[s])

    def t_copy(b):
        part = pl.ds(b * depth, depth)
        return pltpu.make_async_copy(t_hbm.at[:, part], tbuf.at[:, part], tsem.at[b])

    for s in range(sources):
        h_copy(s).start()
    for b in range(blocks):
        t_copy(b).start()
    r[...] = jnp.zeros_like(r)
    for b in range(blocks):
        filled = jnp.int32(0)
        for s in range(sources):
            if b == 0:
                h_copy(s).wait()
            n = count[s * blocks + b]

            def expand(ch, carry, s=s, b=b, filled=filled):
                start = pl.multiple_of(b * slots * lam_each + ch * 4 * lam_each, 4 * lam_each)
                four = hbuf[s, pl.ds(start, 4 * lam_each), :]
                tall = jnp.concatenate([four[:, 128 * j:128 * (j + 1)] for j in range(4)], axis=0)
                y = jnp.dot(tall, wide_vir[b], preferred_element_type=F32)
                for i in range(4):
                    at = filled + ch * 4 + i
                    order[at] = label[(s * blocks + b) * slots + ch * 4 + i]
                    for j in range(4):
                        for e in range(2):
                            z[pl.ds(at * AUXG + 2 * j + e, lam_each, stride=ROWS), :] = y[
                                (j * 4 + i) * lam_each:(j * 4 + i + 1) * lam_each,
                                e * SIG:(e + 1) * SIG,
                            ]
                return carry

            lax.fori_loop(0, (n + 3) // 4, expand, 0)
            filled = filled + n
        t_copy(b).wait()

        def multiply(m, carry, b=b, filled=filled):
            for l in range(lam_each):
                start = pl.multiple_of(l * ROWS + m * 256, 8)
                lhs[:, l * SIG:(l + 1) * SIG] = z[pl.ds(start, 256), :].astype(BF16)
            acc[...] = lax.dot_general(
                lhs[...], tbuf[:, b * depth:(b + 1) * depth],
                (((1,), (1,)), ((), ())), preferred_element_type=F32,
            )

            def scatter(i, inner):
                g = order[m * 32 + i]
                rows = pl.ds(pl.multiple_of(g * AUXG, AUXG), AUXG)
                mine = pl.ds(pl.multiple_of(i * AUXG, AUXG), AUXG)
                for q in range(r.shape[0]):
                    r[q, rows, :] += acc[mine, q * 128:(q + 1) * 128]
                return inner

            lax.fori_loop(0, jnp.minimum(32, filled - m * 32), scatter, 0)
            return carry

        lax.fori_loop(0, (filled + 31) // 32, multiply, 0)

    is_first = core[0] == 0
    low = lax.broadcasted_iota(jnp.int32, (64, 128), 1) < 64
    for a in range(keep_ref.shape[0]):
        for q in range(keep_ref.shape[1]):
            top = r[q, a * 128:a * 128 + 64, :]
            bottom = r[q, a * 128 + 64:a * 128 + 128, :]
            even = jnp.where(low, top, pltpu.roll(bottom, 64, 1))
            odd = jnp.where(low, pltpu.roll(top, 64, 1), bottom)
            keep_ref[a, q] = jnp.where(is_first, even, odd)
            send_ref[a, q] = jnp.where(is_first, odd, even).astype(BF16)


def local(three_centre, slot_groups, slot_count, block_cost, green_occ, green_vir, target):
    blocks, slots = slot_groups.shape
    dests = lax.axis_size("aux")
    chips = lax.axis_size("chip")
    lam_each = LAM // dests
    smem = pl.BlockSpec(memory_space=pltpu.SMEM)
    vmem = pl.BlockSpec(memory_space=pltpu.VMEM)
    anywhere = pl.BlockSpec(memory_space=pl.ANY)

    header = jnp.zeros((lam_each, AUXG * NU), BF16)
    table = jnp.concatenate([slot_groups.reshape(-1), slot_count.reshape(-1)])
    header = header.at[0, :table.shape[0]].set(table.astype(BF16))
    rows = blocks * slots * lam_each + lam_each
    sent = pl.pallas_call(
        half_kernel,
        out_shape=jax.ShapeDtypeStruct((dests, rows, AUXG * NU), BF16),
        in_specs=[smem, smem, anywhere, vmem, vmem],
        out_specs=vmem,
        scratch_shapes=[
            pltpu.VMEM((DEPTH, AUXG, NU, MU), BF16),
            pltpu.SemaphoreType.DMA((DEPTH,)),
        ],
        name="half",
    )(slot_count.reshape(-1), block_cost.reshape(-1), three_centre, green_occ, header)
    arrived = lax.all_to_all(sent, "aux", split_axis=0, concat_axis=0, tiled=True)

    tables = arrived[:, rows - lam_each, :table.shape[0]].astype(jnp.int32)
    labels = tables[:, :blocks * slots].reshape(-1)
    counts = tables[:, blocks * slots:].reshape(-1)
    columns = target.reshape(NAUX, -1)
    nothing = jnp.zeros_like(green_vir)
    wide_vir = jnp.concatenate(
        [
            jnp.concatenate([green_vir, nothing], axis=2),
            jnp.concatenate([nothing, green_vir], axis=2),
        ],
        axis=1,
    )
    core = lax.axis_index("core").reshape(1)
    keep, send = pl.pallas_call(
        response_kernel,
        out_shape=(
            jax.ShapeDtypeStruct((dests, chips, 64, 128), F32),
            jax.ShapeDtypeStruct((dests, chips, 64, 128), BF16),
        ),
        in_specs=[smem, smem, smem, anywhere, vmem, anywhere],
        out_specs=(vmem, vmem),
        scratch_shapes=[
            pltpu.VMEM((dests, blocks * slots * lam_each, AUXG * NU), BF16),
            pltpu.VMEM(columns.shape, BF16),
            pltpu.VMEM((lam_each * ROWS, SIG), F32),
            pltpu.VMEM((256, lam_each * SIG), BF16),
            pltpu.VMEM((256, NAUX), F32),
            pltpu.VMEM((NAUX // 128, NAUX, 128), F32),
            pltpu.SMEM((NGROUPS + 4,), jnp.int32),
            pltpu.SemaphoreType.DMA((dests,)),
            pltpu.SemaphoreType.DMA((blocks,)),
        ],
        name="response",
    )(counts, labels, core, arrived, wide_vir, columns)
    other = lax.ppermute(send, "core", [(0, 1), (1, 0)])
    mine = (keep + other.astype(F32)).astype(BF16).reshape(dests * chips, 64, 128)
    parts = lax.all_to_all(mine, ("aux", "chip"), split_axis=0, concat_axis=0, tiled=True)
    total = jnp.sum(parts.astype(F32), axis=0)
    return jnp.concatenate([total[:, :64], total[:, 64:]], axis=0)


def solution(mesh):
    aux, pair = mesh.devices.shape
    fine = jax.sharding.Mesh(
        mesh.devices.reshape(aux, pair // 2, 2), ("aux", "chip", "core")
    )
    both = ("chip", "core")
    in_specs = (
        P(both, "aux", None, None, None),
        P(both, "aux"),
        P(both, "aux"),
        P(both, "aux"),
        P(both, None, None),
        P(both, None, None),
        P(None, both, "aux", None),
    )
    return jax.shard_map(local, mesh=fine, in_specs=in_specs, out_specs=P("aux", both), check_vma=False)
```

```python
import functools

import jax
import jax.numpy as jnp
from jax import lax
from jax.experimental import pallas as pl
from jax.experimental.pallas import tpu as pltpu
from jax.sharding import PartitionSpec as P


NAUX = 1024
AUXG = 8
MU = 512
NU = 64
LAM = 128
SIG = 128
MUC = 128
NGROUPS = 128
DEPTH = 4
CHUNKS = 2
AUXC = AUXG // CHUNKS
BF16 = jnp.bfloat16
F32 = jnp.float32


def fold(low, first, second):
    return (
        jnp.where(low, first, pltpu.roll(second, 64, 1)),
        jnp.where(low, pltpu.roll(first, 64, 1), second),
    )


def half_kernel(chunk, dests, count, cost, group, me, x_hbm, occ, *rest):
    outs, (xbuf, turned, sem) = rest[:dests], rest[dests:]
    blocks, slots = cost.shape
    units = MU // MUC
    shape = (8, 128)
    row = lax.broadcasted_iota(jnp.int32, shape, 0)
    lane = lax.broadcasted_iota(jnp.int32, shape, 1)
    low = lane < 64
    head = jnp.zeros(shape, jnp.int32)
    for b in range(blocks):
        head = jnp.where((row == b) & (lane == slots), count[b, 0], head)
        for s in range(slots):
            head = jnp.where((row == b) & (lane == s), group[b, s], head)
    head = head.astype(F32).astype(BF16)
    for out in outs:
        out[blocks * slots, :, 0:128] = head
    first = count[0, 0]
    total = first + count[1, 0]

    def place(i):
        b = jnp.where(i < first, 0, 1)
        return b, i - b * first

    def copy(i, k):
        b, s = place(i)
        slot = lax.rem(i, DEPTH)
        return pltpu.make_async_copy(
            x_hbm.at[b, s, pl.ds(chunk * AUXC, AUXC), :, pl.ds(0, MUC * k)],
            xbuf.at[slot, :, :, pl.ds(0, MUC * k)],
            sem.at[slot],
        )

    def issue(i):
        b, s = place(i)
        c = cost[b, s]
        for k in range(1, units + 1):
            @pl.when(c == k)
            def _(k=k):
                copy(i, k).start()

    for i in range(DEPTH - 1):
        @pl.when(i < total)
        def _(i=i):
            issue(i)

    def step(i, carry):
        b, s = place(i)
        slot = lax.rem(i, DEPTH)

        @pl.when(i + DEPTH - 1 < total)
        def _():
            issue(i + DEPTH - 1)

        c = cost[b, s]
        for k in range(1, units + 1):
            @pl.when(c == k)
            def _(k=k):
                copy(i, k).wait()
                x = xbuf[slot, :, :, 0:MUC * k].reshape(AUXC * NU, MUC * k)
                h = jnp.dot(x, occ[b, 0:MUC * k, :], preferred_element_type=F32)
                turned[...] = h.T.reshape(turned.shape)
        for d in range(dests):
            mine = turned[me[0] ^ d]
            parts = []
            for j in range(AUXC // 2):
                cols = slice(128 * j, 128 * (j + 1))
                parts += fold(low, mine[0:8, cols], mine[8:16, cols])
            outs[d][b * slots + s] = jnp.concatenate(parts, axis=1).astype(BF16)
        return carry

    lax.fori_loop(0, total, step, 0)


ROWS = NGROUPS * AUXC + 16


def response_kernel(sources, core, *rest):
    parts, rest = rest[:sources], rest[sources:]
    t_hbm, keep_ref, send_ref, tbuf, z, lhs, acc, r, headint, table, order, tsem, ssem = rest
    blocks = t_hbm.shape[0]
    pairs = LAM // sources // 2
    slots = NGROUPS // sources
    block_rows = 256
    held = block_rows // AUXC

    def t_copy(b):
        return pltpu.make_async_copy(t_hbm.at[b], tbuf.at[b], tsem.at[b])

    for b in range(blocks):
        t_copy(b).start()
    for s in range(sources):
        headint[s] = parts[s][blocks * slots, :, 0:128].astype(F32).astype(jnp.int32)
    to_scalar = pltpu.make_async_copy(headint, table, ssem.at[0])
    to_scalar.start()
    r[...] = jnp.zeros_like(r)
    half_tile = lax.broadcasted_iota(jnp.int32, (8, 128), 0) // AUXC
    to_scalar.wait()
    for b in range(blocks):
        filled = jnp.int32(0)
        for s in range(sources):
            n = table[s, b, slots]

            def spread(ch, carry, s=s, b=b, filled=filled):
                for i in range(4):
                    at = filled + ch * 4 + i
                    order[at] = table[s, b, ch * 4 + i]
                    one = parts[s][b * slots + ch * 4 + i].astype(F32)
                    for a in range(AUXC):
                        z[pl.ds(at * AUXC + a, pairs, stride=ROWS), :] = one[:, 128 * a:128 * (a + 1)]
                return carry

            lax.fori_loop(0, (n + 3) // 4, spread, 0)
            filled = filled + n
        t_copy(b).wait()

        def multiply(m, carry, b=b, filled=filled):
            for q in range(pairs):
                start = pl.multiple_of(q * ROWS + m * block_rows, 8)
                lhs[:, q * 128:(q + 1) * 128] = z[pl.ds(start, block_rows), :].astype(BF16)
            acc[...] = lax.dot_general(
                lhs[...], tbuf[b], (((1,), (1,)), ((), ())), preferred_element_type=F32,
            )

            def scatter(i, inner):
                g = order[m * held + i]
                mask = half_tile == lax.rem(g, 2)
                turn = lax.rem(g + i, 2) == 1
                to = pl.ds(pl.multiple_of((g // 2) * 8, 8), 8)
                at = pl.ds(pl.multiple_of((i // 2) * 8, 8), 8)
                for q in range(r.shape[0]):
                    v = acc[at, q * 128:(q + 1) * 128]
                    v = jnp.where(turn, pltpu.roll(v, 4, 0), v)
                    r[q, to, :] += jnp.where(mask, v, 0.0)
                return inner

            lax.fori_loop(0, jnp.minimum(held, filled - m * held), scatter, 0)
            return carry

        lax.fori_loop(0, (filled + held - 1) // held, multiply, 0)

    is_first = core[0] == 0
    height = keep_ref.shape[2]
    low = lax.broadcasted_iota(jnp.int32, (height, 128), 1) < 64
    for a in range(keep_ref.shape[0]):
        for q in range(keep_ref.shape[1]):
            at = 2 * height * a
            even, odd = fold(low, r[q, at:at + height, :], r[q, at + height:at + 2 * height, :])
            keep_ref[a, q] = jnp.where(is_first, even, odd)
            send_ref[a, q] = jnp.where(is_first, odd, even).astype(BF16)


def local(three_centre, slot_groups, slot_count, block_cost, green_occ, green_vir, target):
    blocks, slots = slot_groups.shape
    dests = lax.axis_size("aux")
    chips = lax.axis_size("chip")
    pairs = LAM // dests // 2
    smem = pl.BlockSpec(memory_space=pltpu.SMEM)
    vmem = pl.BlockSpec(memory_space=pltpu.VMEM)
    anywhere = pl.BlockSpec(memory_space=pltpu.MemorySpace.HBM)
    height = NAUX // dests // CHUNKS // 2

    me = lax.axis_index("aux").reshape(1)
    arrived = []
    for chunk in range(CHUNKS):
        held = blocks * slots + 1
        sent = pl.pallas_call(
            functools.partial(half_kernel, chunk, dests),
            out_shape=[jax.ShapeDtypeStruct((held, pairs, AUXC * 128), BF16)] * dests,
            in_specs=[smem, smem, smem, smem, anywhere, vmem],
            out_specs=[vmem] * dests,
            scratch_shapes=[
                pltpu.VMEM((DEPTH, AUXC, NU, MU), BF16),
                pltpu.VMEM((dests, LAM // dests, AUXC * NU), F32),
                pltpu.SemaphoreType.DMA((DEPTH,)),
            ],
            cost_estimate=pl.CostEstimate(flops=10**9, bytes_accessed=10**7, transcendentals=0),
        )(slot_count, block_cost, slot_groups, me, three_centre, green_occ)
        arrived.append([sent[0]] + [
            lax.ppermute(sent[d], "aux", [(i, i ^ d) for i in range(dests)])
            for d in range(1, dests)
        ])

    target, ready = lax.optimization_barrier((target, sent[0]))
    arrived[-1][0] = ready
    columns = jnp.einsum(
        "qbzit,bnt->bqizn", target.reshape(NAUX, blocks, 2, pairs, SIG), green_vir,
        preferred_element_type=F32,
    ).astype(BF16).reshape(blocks, NAUX, pairs * 128)
    core = lax.axis_index("core").reshape(1)
    pieces = []
    mine = None
    for chunk in range(CHUNKS):
        if mine is not None:
            core, mine = lax.optimization_barrier((core, mine))
            pieces[-1] = mine
        respond = pl.pallas_call(
            functools.partial(response_kernel, dests),
            out_shape=(
                jax.ShapeDtypeStruct((dests, chips, height, 128), F32),
                jax.ShapeDtypeStruct((dests, chips, height, 128), BF16),
            ),
            in_specs=[smem] + [vmem] * dests + [anywhere],
            out_specs=(vmem, vmem),
            scratch_shapes=[
                pltpu.VMEM((blocks, NAUX, pairs * 128), BF16),
                pltpu.VMEM((pairs * ROWS, 128), F32),
                pltpu.VMEM((256, pairs * 128), BF16),
                pltpu.VMEM((256, NAUX), F32),
                pltpu.VMEM((NAUX // 128, NGROUPS * AUXC, 128), F32),
                pltpu.VMEM((dests, 8, 128), jnp.int32),
                pltpu.SMEM((dests, 8, 128), jnp.int32),
                pltpu.SMEM((NGROUPS + 4,), jnp.int32),
                pltpu.SemaphoreType.DMA((blocks,)),
                pltpu.SemaphoreType.DMA((1,)),
            ],
            cost_estimate=pl.CostEstimate(flops=3 * 10**9, bytes_accessed=10**7, transcendentals=0),
            compiler_params=pltpu.CompilerParams(vmem_limit_bytes=24 * 2**20),
        )
        keep, send = respond(core, *arrived[chunk], columns)
        other = lax.ppermute(send, "core", [(0, 1), (1, 0)])
        mine = (keep + other.astype(F32)).astype(BF16).reshape(dests * chips, height, 128)
        pieces.append(mine)
    results = []
    for mine in pieces:
        parts = lax.all_to_all(mine, ("aux", "chip"), split_axis=0, concat_axis=0, tiled=True)
        total = jnp.sum(parts.astype(F32), axis=0)
        total = jnp.concatenate([total[:, :64], total[:, 64:]], axis=0)
        results.append(total.reshape(-1, AUXC, 64))
    return jnp.concatenate(results, axis=1).reshape(-1, 64)


def solution(mesh):
    aux, pair = mesh.devices.shape
    fine = jax.sharding.Mesh(
        mesh.devices.reshape(aux, pair // 2, 2), ("aux", "chip", "core")
    )
    both = ("chip", "core")
    in_specs = (
        P(both, "aux", None, None, None),
        P(both, "aux"),
        P(both, "aux"),
        P(both, "aux"),
        P(both, None, None),
        P(both, None, None),
        P(None, both, "aux", None),
    )

    return jax.shard_map(local, mesh=fine, in_specs=in_specs, out_specs=P("aux", both), check_vma=False)
```

```python
import functools

import jax
import jax.numpy as jnp
from jax import lax
from jax.experimental import pallas as pl
from jax.experimental.pallas import tpu as pltpu
from jax.sharding import PartitionSpec as P


NAUX = 1024
AUXG = 8
MU = 512
NU = 64
LAM = 128
SIG = 128
MUC = 128
NGROUPS = 128
DEPTH = 4
BF16 = jnp.bfloat16
F32 = jnp.float32
STAGES = ((0, 2, 6, 1, 5), (3, 7, 4))


def fold(low, first, second):
    return (
        jnp.where(low, first, pltpu.roll(second, 64, 1)),
        jnp.where(low, pltpu.roll(first, 64, 1), second),
    )


def half_kernel(dests, count, cost, group, me, x_hbm, occ, *rest):
    outs, (xbuf, turned, sem) = rest[:dests], rest[dests:]
    blocks, slots = cost.shape
    lam_each = LAM // dests
    units = MU // MUC
    first = count[0]
    total = first + count[1]

    def place(i):
        b = jnp.where(i < first, 0, 1)
        return b, i - b * first

    def copy(i, k):
        b, s = place(i)
        slot = lax.rem(i, DEPTH)
        return pltpu.make_async_copy(
            x_hbm.at[b, s, :, :, pl.ds(0, MUC * k)],
            xbuf.at[slot, :, :, pl.ds(0, MUC * k)],
            sem.at[slot],
        )

    def issue(i):
        b, s = place(i)
        c = cost[b, s]
        for k in range(1, units + 1):
            @pl.when(c == k)
            def _(k=k):
                copy(i, k).start()

    for i in range(DEPTH - 1):
        @pl.when(i < total)
        def _(i=i):
            issue(i)

    shape = (lam_each, 128)
    row = lax.broadcasted_iota(jnp.int32, shape, 0)
    lane = lax.broadcasted_iota(jnp.int32, shape, 1)
    head = jnp.zeros(shape, jnp.int32)
    for b in range(blocks):
        head = jnp.where((row == b) & (lane == slots), count[b], head)
        for s in range(slots):
            head = jnp.where((row == b) & (lane == s), group[b, s], head)
    head = head.astype(F32).astype(BF16)
    for out in outs:
        out[blocks * slots * lam_each:, 0:128] = head
    old = lax.broadcasted_iota(jnp.int32, (LAM, LAM), 0)
    new = lax.broadcasted_iota(jnp.int32, (LAM, LAM), 1)
    moves = old == (me[0] ^ (new // lam_each)) * lam_each + lax.rem(new, lam_each)
    moves = jnp.where(moves, 1.0, 0.0).astype(BF16)
    for b in range(blocks):
        turned[b] = jnp.dot(occ[b], moves, preferred_element_type=F32).astype(BF16)

    def step(i, carry):
        b, s = place(i)
        slot = lax.rem(i, DEPTH)

        @pl.when(i + DEPTH - 1 < total)
        def _():
            issue(i + DEPTH - 1)

        c = cost[b, s]
        for k in range(1, units + 1):
            @pl.when(c == k)
            def _(k=k):
                copy(i, k).wait()
                x = xbuf[slot, :, :, 0:MUC * k].reshape(AUXG * NU, MUC * k)
                h = jnp.dot(x, turned[b, 0:MUC * k, :], preferred_element_type=F32)
                ht = h.T.astype(BF16)
                at = pl.multiple_of((b * slots + s) * lam_each, lam_each)
                for d in range(dests):
                    outs[d][pl.ds(at, lam_each), :] = ht[d * lam_each:(d + 1) * lam_each]
        return carry

    lax.fori_loop(0, total, step, 0)


ROWS = NAUX + 32


def response_kernel(sources, last, *rest):
    if last:
        core, rest = rest[0], rest[1:]
    parts, rest = rest[:sources], rest[sources:]
    if last:
        before, columns, keep_ref, send_ref, z, lhs, acc, headint, table, order, ssem, r = rest
    else:
        columns, r, z, lhs, acc, headint, table, order, ssem = rest
    blocks, _, width = columns.shape
    pairs = width // 128
    lam_each = 2 * pairs
    slots = (parts[0].shape[0] - lam_each) // (blocks * lam_each)
    block_rows = 256
    held = block_rows // AUXG

    for s in range(sources):
        rows = parts[s][blocks * slots * lam_each:, 0:128]
        headint[s] = rows.astype(F32).astype(jnp.int32)[0:8]
    to_scalar = pltpu.make_async_copy(headint, table, ssem.at[0])
    to_scalar.start()
    r[...] = before[...] if last else jnp.zeros_like(r)
    low = lax.broadcasted_iota(jnp.int32, (8, 128), 1) < 64
    to_scalar.wait()
    for b in range(blocks):
        filled = jnp.int32(0)
        for s in range(sources):
            n = table[s, b, slots]

            def spread(ch, carry, s=s, b=b, filled=filled):
                start = pl.multiple_of((b * slots + ch * 4) * lam_each, 4 * lam_each)
                four = parts[s][pl.ds(start, 4 * lam_each), :].astype(F32)
                for i in range(4):
                    at = filled + ch * 4 + i
                    order[at] = table[s, b, ch * 4 + i]
                    for j in range(AUXG // 2):
                        cols = slice(128 * j, 128 * (j + 1))
                        upper = four[i * lam_each:i * lam_each + pairs, cols]
                        lower = four[i * lam_each + pairs:(i + 1) * lam_each, cols]
                        for e, v in enumerate(fold(low, upper, lower)):
                            z[pl.ds(at * AUXG + 2 * j + e, pairs, stride=ROWS), :] = v
                return carry

            lax.fori_loop(0, (n + 3) // 4, spread, 0)
            filled = filled + n

        def multiply(m, carry, b=b, filled=filled):
            for q in range(pairs):
                start = pl.multiple_of(q * ROWS + m * block_rows, 8)
                lhs[:, q * 128:(q + 1) * 128] = z[pl.ds(start, block_rows), :].astype(BF16)
            acc[...] = lax.dot_general(
                lhs[...], columns[b], (((1,), (1,)), ((), ())), preferred_element_type=F32,
            )

            def scatter(i, inner):
                g = order[m * held + i]
                to = pl.ds(pl.multiple_of(g * AUXG, AUXG), AUXG)
                at = pl.ds(pl.multiple_of(i * AUXG, AUXG), AUXG)
                for q in range(r.shape[0]):
                    r[q, to, :] += acc[at, q * 128:(q + 1) * 128]
                return inner

            lax.fori_loop(0, jnp.minimum(held, filled - m * held), scatter, 0)
            return carry

        lax.fori_loop(0, (filled + held - 1) // held, multiply, 0)

    if last:
        is_first = core[0] == 0
        low = lax.broadcasted_iota(jnp.int32, (64, 128), 1) < 64
        for a in range(keep_ref.shape[0]):
            for q in range(keep_ref.shape[1]):
                even, odd = fold(
                    low, r[q, a * 128:a * 128 + 64, :], r[q, a * 128 + 64:a * 128 + 128, :])
                keep_ref[a, q] = jnp.where(is_first, even, odd)
                send_ref[a, q] = jnp.where(is_first, odd, even).astype(BF16)


def local(three_centre, slot_groups, slot_count, block_cost, green_occ, green_vir, target):
    blocks, slots = slot_groups.shape
    dests = lax.axis_size("aux")
    chips = lax.axis_size("chip")
    lam_each = LAM // dests
    pairs = lam_each // 2
    smem = pl.BlockSpec(memory_space=pltpu.SMEM)
    vmem = pl.BlockSpec(memory_space=pltpu.VMEM)
    hbm = pl.BlockSpec(memory_space=pltpu.MemorySpace.HBM)

    held = (blocks * slots + 1) * lam_each
    sent = pl.pallas_call(
        functools.partial(half_kernel, dests),
        out_shape=[jax.ShapeDtypeStruct((held, AUXG * NU), BF16)] * dests,
        in_specs=[smem, smem, smem, smem, hbm, vmem],
        out_specs=[vmem] * dests,
        scratch_shapes=[
            pltpu.VMEM((DEPTH, AUXG, NU, MU), BF16),
            pltpu.VMEM((blocks, MU, LAM), BF16),
            pltpu.SemaphoreType.DMA((DEPTH,)),
        ],
        cost_estimate=pl.CostEstimate(flops=2 * 10**9, bytes_accessed=2 * 10**7, transcendentals=0),
        name="half",
    )(slot_count.reshape(-1), block_cost, slot_groups, lax.axis_index("aux").reshape(1),
      three_centre, green_occ)
    arrived = {0: sent[0]}
    for stage in STAGES:
        for d in stage:
            if d:
                arrived[d] = lax.ppermute(sent[d], "aux", [(i, i ^ d) for i in range(dests)])

    columns = jnp.einsum(
        "qbzit,bnt->bqizn", target.reshape(NAUX, blocks, 2, pairs, SIG), green_vir,
        preferred_element_type=F32,
    ).astype(BF16).reshape(blocks, NAUX, pairs * 128)
    core = lax.axis_index("core").reshape(1)
    running = None
    for number, stage in enumerate(STAGES):
        last = number == len(STAGES) - 1
        inputs = [arrived[d] for d in stage]
        specs = [vmem] * len(stage)
        whole = jax.ShapeDtypeStruct((NAUX // 128, NAUX, 128), F32)
        scratch = [
            pltpu.VMEM((pairs * ROWS, 128), F32),
            pltpu.VMEM((256, pairs * 128), BF16),
            pltpu.VMEM((256, NAUX), F32),
            pltpu.VMEM((len(stage), 8, 128), jnp.int32),
            pltpu.SMEM((len(stage), 8, 128), jnp.int32),
            pltpu.SMEM((NGROUPS + 4,), jnp.int32),
            pltpu.SemaphoreType.DMA((1,)),
        ]
        shape = whole
        if last:
            inputs = [core, *inputs, running]
            specs = [smem, *specs, vmem]
            scratch.append(pltpu.VMEM(whole.shape, F32))
            shape = (
                jax.ShapeDtypeStruct((dests, chips, 64, 128), F32),
                jax.ShapeDtypeStruct((dests, chips, 64, 128), BF16),
            )
        respond = pl.pallas_call(
            functools.partial(response_kernel, len(stage), last),
            out_shape=shape,
            in_specs=[*specs, vmem],
            out_specs=(vmem, vmem) if last else vmem,
            scratch_shapes=scratch,
            compiler_params=pltpu.CompilerParams(vmem_limit_bytes=24 * 2**20),
            cost_estimate=pl.CostEstimate(flops=3 * 10**9, bytes_accessed=10**7, transcendentals=0),
        )
        running = respond(*inputs, columns)
    keep, send = running
    other = lax.ppermute(send, "core", [(0, 1), (1, 0)])
    mine = (keep + other.astype(F32)).astype(BF16).reshape(dests * chips, 64, 128)
    parts = lax.all_to_all(mine, ("aux", "chip"), split_axis=0, concat_axis=0, tiled=True)
    total = jnp.sum(parts.astype(F32), axis=0)
    return jnp.concatenate([total[:, :64], total[:, 64:]], axis=0)


def solution(mesh):
    aux, pair = mesh.devices.shape
    fine = jax.sharding.Mesh(
        mesh.devices.reshape(aux, pair // 2, 2), ("aux", "chip", "core")
    )
    both = ("chip", "core")
    in_specs = (
        P(both, "aux", None, None, None),
        P(both, "aux"),
        P(both, "aux"),
        P(both, "aux"),
        P(both, None, None),
        P(both, None, None),
        P(None, both, "aux", None),
    )

    return jax.shard_map(local, mesh=fine, in_specs=in_specs, out_specs=P("aux", both), check_vma=False)
```

```python
import functools

import jax
import jax.numpy as jnp
from jax import lax
from jax.experimental import pallas as pl
from jax.experimental.pallas import tpu as pltpu
from jax.sharding import PartitionSpec as P


NAUX = 1024
AUXG = 8
MU = 512
NU = 64
LAM = 128
SIG = 128
MUC = 128
NGROUPS = 128
DEPTH = 6
BF16 = jnp.bfloat16
F32 = jnp.float32
STAGES = ((0, 1, 2, 5, 6, 3, 4), (7,))


def fold(low, first, second):
    return (
        jnp.where(low, first, pltpu.roll(second, 64, 1)),
        jnp.where(low, pltpu.roll(first, 64, 1), second),
    )


def half_kernel(dests, count, cost, group, me, x_hbm, occ, *rest):
    outs, (xbuf, turned, sem) = rest[:dests], rest[dests:]
    blocks, slots = cost.shape
    lam_each = LAM // dests
    units = MU // MUC
    first = count[0]
    total = first + count[1]

    def place(i):
        b = jnp.where(i < first, 0, 1)
        return b, i - b * first

    def copy(i, k):
        b, s = place(i)
        slot = lax.rem(i, DEPTH)
        return pltpu.make_async_copy(
            x_hbm.at[b, s, :, :, pl.ds(0, MUC * k)],
            xbuf.at[slot, :, :, pl.ds(0, MUC * k)],
            sem.at[slot],
        )

    def each_size(i, act):
        b, s = place(i)
        c = jnp.where(i < DEPTH, units, cost[b, s])
        for k in range(1, units + 1):
            @pl.when((c == k) & (i < total))
            def _(k=k):
                act(copy(i, k))

    def issue(i):
        each_size(i, lambda c: c.start())

    for i in range(DEPTH - 2):
        issue(i)

    shape = (lam_each, 128)
    row = lax.broadcasted_iota(jnp.int32, shape, 0)
    lane = lax.broadcasted_iota(jnp.int32, shape, 1)
    head = jnp.zeros(shape, jnp.int32)
    for b in range(blocks):
        head = jnp.where((row == b) & (lane == slots), count[b], head)
        for s in range(slots):
            head = jnp.where((row == b) & (lane == s), group[b, s], head)
    head = head.astype(F32).astype(BF16)
    for out in outs:
        out[blocks * slots * lam_each:, 0:128] = head
    old = lax.broadcasted_iota(jnp.int32, (LAM, LAM), 0)
    new = lax.broadcasted_iota(jnp.int32, (LAM, LAM), 1)
    moves = old == (me[0] ^ (new // lam_each)) * lam_each + lax.rem(new, lam_each)
    moves = jnp.where(moves, 1.0, 0.0).astype(BF16)
    for b in range(blocks):
        whole = jnp.dot(occ[b], moves, preferred_element_type=F32).astype(BF16)
        for k in range(1, units + 1):
            turned[k - 1, b, 0:MUC * k] = whole[0:MUC * k]
            if k < units:
                turned[k - 1, b, MUC * k:] = jnp.zeros_like(whole[MUC * k:])

    def step(t, carry):
        for i in (2 * t, 2 * t + 1):
            each_size(i, lambda c: c.wait())
            issue(i + DEPTH - 2)
        for i in (2 * t, jnp.minimum(2 * t + 1, total - 1)):
            b, s = place(i)
            x = xbuf[lax.rem(i, DEPTH)].reshape(AUXG * NU, MU)
            h = jnp.dot(x, turned[cost[b, s] - 1, b], preferred_element_type=F32)
            ht = h.T.astype(BF16)
            at = pl.multiple_of((b * slots + s) * lam_each, lam_each)
            for d in range(dests):
                outs[d][pl.ds(at, lam_each), :] = ht[d * lam_each:(d + 1) * lam_each]
        return carry

    lax.fori_loop(0, (total + 1) // 2, step, 0)


def response_kernel(sources, last, *rest):
    if last:
        core, rest = rest[0], rest[1:]
    parts, rest = rest[:sources], rest[sources:]
    if last:
        before, columns, keep_ref, send_ref, z, lhs, acc, headint, table, order, ssem, r = rest
    else:
        columns, r, z, lhs, acc, headint, table, order, ssem = rest
    blocks, _, width = columns.shape
    pairs = width // 128
    lam_each = 2 * pairs
    slots = (parts[0].shape[0] - lam_each) // (blocks * lam_each)
    block_rows = lhs.shape[0]
    held = block_rows // AUXG
    reach = z.shape[0] // pairs

    for s in range(sources):
        rows = parts[s][blocks * slots * lam_each:, 0:128]
        headint[s] = rows.astype(F32).astype(jnp.int32)[0:8]
    to_scalar = pltpu.make_async_copy(headint, table, ssem.at[0])
    to_scalar.start()
    r[...] = before[...] if last else jnp.zeros_like(r)
    low = lax.broadcasted_iota(jnp.int32, (8, 128), 1) < 64
    to_scalar.wait()
    for b in range(blocks):
        filled = jnp.int32(0)
        for s in range(sources):
            n = table[s, b, slots]

            def spread(ch, carry, s=s, b=b, filled=filled):
                start = pl.multiple_of((b * slots + ch * 4) * lam_each, 4 * lam_each)
                four = parts[s][pl.ds(start, 4 * lam_each), :].astype(F32)
                for i in range(4):
                    at = filled + ch * 4 + i
                    order[at] = table[s, b, ch * 4 + i]
                    for j in range(AUXG // 2):
                        cols = slice(128 * j, 128 * (j + 1))
                        upper = four[i * lam_each:i * lam_each + pairs, cols]
                        lower = four[i * lam_each + pairs:(i + 1) * lam_each, cols]
                        for e, v in enumerate(fold(low, upper, lower)):
                            z[pl.ds(at * AUXG + 2 * j + e, pairs, stride=reach), :] = v
                return carry

            lax.fori_loop(0, (n + 3) // 4, spread, 0)
            filled = filled + n

        def multiply(m, carry, b=b, filled=filled):
            for q in range(pairs):
                start = pl.multiple_of(q * reach + m * block_rows, 8)
                lhs[:, q * 128:(q + 1) * 128] = z[pl.ds(start, block_rows), :].astype(BF16)
            acc[...] = lax.dot_general(
                lhs[...], columns[b], (((1,), (1,)), ((), ())), preferred_element_type=F32,
            )

            def scatter(i, inner):
                g = order[m * held + i]
                to = pl.ds(pl.multiple_of(g * AUXG, AUXG), AUXG)
                at = pl.ds(pl.multiple_of(i * AUXG, AUXG), AUXG)
                for q in range(r.shape[0]):
                    r[q, to, :] += acc[at, q * 128:(q + 1) * 128]
                return inner

            lax.fori_loop(0, jnp.minimum(held, filled - m * held), scatter, 0)
            return carry

        lax.fori_loop(0, (filled + held - 1) // held, multiply, 0)

    if last:
        is_first = core[0] == 0
        low = lax.broadcasted_iota(jnp.int32, (64, 128), 1) < 64
        for a in range(keep_ref.shape[0]):
            for q in range(keep_ref.shape[1]):
                even, odd = fold(
                    low, r[q, a * 128:a * 128 + 64, :], r[q, a * 128 + 64:a * 128 + 128, :])
                keep_ref[a, q] = jnp.where(is_first, even, odd)
                send_ref[a, q] = jnp.where(is_first, odd, even).astype(BF16)


def local(three_centre, slot_groups, slot_count, block_cost, green_occ, green_vir, target):
    blocks, slots = slot_groups.shape
    dests = lax.axis_size("aux")
    chips = lax.axis_size("chip")
    lam_each = LAM // dests
    pairs = lam_each // 2
    smem = pl.BlockSpec(memory_space=pltpu.SMEM)
    vmem = pl.BlockSpec(memory_space=pltpu.VMEM)
    hbm = pl.BlockSpec(memory_space=pltpu.MemorySpace.HBM)

    held = (blocks * slots + 1) * lam_each
    sent = pl.pallas_call(
        functools.partial(half_kernel, dests),
        out_shape=[jax.ShapeDtypeStruct((held, AUXG * NU), BF16)] * dests,
        in_specs=[smem, smem, smem, smem, hbm, vmem],
        out_specs=[vmem] * dests,
        scratch_shapes=[
            pltpu.VMEM((DEPTH, AUXG, NU, MU), BF16),
            pltpu.VMEM((MU // MUC, blocks, MU, LAM), BF16),
            pltpu.SemaphoreType.DMA((DEPTH,)),
        ],
        cost_estimate=pl.CostEstimate(flops=2 * 10**9, bytes_accessed=2 * 10**7, transcendentals=0),
        name="half",
    )(slot_count.reshape(-1), block_cost, slot_groups, lax.axis_index("aux").reshape(1),
      three_centre, green_occ)
    arrived = {0: sent[0]}
    for stage in STAGES:
        for d in stage:
            if d:
                arrived[d] = lax.ppermute(sent[d], "aux", [(i, i ^ d) for i in range(dests)])

    columns = jnp.einsum(
        "qbzit,bnt->bqizn", target.reshape(NAUX, blocks, 2, pairs, SIG), green_vir,
        preferred_element_type=F32,
    ).astype(BF16).reshape(blocks, NAUX, pairs * 128)
    core = lax.axis_index("core").reshape(1)
    running = None
    for number, stage in enumerate(STAGES):
        last = number == len(STAGES) - 1
        most = len(stage) * slots * AUXG
        block_rows = min(256, most)
        reach = -(-most // block_rows) * block_rows + 32
        inputs = [arrived[d] for d in stage]
        specs = [vmem] * len(stage)
        whole = jax.ShapeDtypeStruct((NAUX // 128, NAUX, 128), F32)
        scratch = [
            pltpu.VMEM((pairs * reach, 128), F32),
            pltpu.VMEM((block_rows, pairs * 128), BF16),
            pltpu.VMEM((block_rows, NAUX), F32),
            pltpu.VMEM((len(stage), 8, 128), jnp.int32),
            pltpu.SMEM((len(stage), 8, 128), jnp.int32),
            pltpu.SMEM((NGROUPS + 4,), jnp.int32),
            pltpu.SemaphoreType.DMA((1,)),
        ]
        shape = whole
        if last:
            inputs = [core, *inputs, running]
            specs = [smem, *specs, vmem]
            scratch.append(pltpu.VMEM(whole.shape, F32))
            shape = (
                jax.ShapeDtypeStruct((dests, chips, 64, 128), F32),
                jax.ShapeDtypeStruct((dests, chips, 64, 128), BF16),
            )
        respond = pl.pallas_call(
            functools.partial(response_kernel, len(stage), last),
            out_shape=shape,
            in_specs=[*specs, vmem],
            out_specs=(vmem, vmem) if last else vmem,
            scratch_shapes=scratch,
            compiler_params=pltpu.CompilerParams(vmem_limit_bytes=24 * 2**20),
            cost_estimate=pl.CostEstimate(flops=3 * 10**9, bytes_accessed=10**7, transcendentals=0),
        )
        running = respond(*inputs, columns)
    keep, send = running
    other = lax.ppermute(send, "core", [(0, 1), (1, 0)])
    mine = (keep + other.astype(F32)).astype(BF16).reshape(dests * chips, 64, 128)
    parts = lax.all_to_all(mine, ("aux", "chip"), split_axis=0, concat_axis=0, tiled=True)
    total = jnp.sum(parts.astype(F32), axis=0)
    return jnp.concatenate([total[:, :64], total[:, 64:]], axis=0)


def solution(mesh):
    aux, pair = mesh.devices.shape
    fine = jax.sharding.Mesh(
        mesh.devices.reshape(aux, pair // 2, 2), ("aux", "chip", "core")
    )
    both = ("chip", "core")
    in_specs = (
        P(both, "aux", None, None, None),
        P(both, "aux"),
        P(both, "aux"),
        P(both, "aux"),
        P(both, None, None),
        P(both, None, None),
        P(None, both, "aux", None),
    )

    return jax.shard_map(local, mesh=fine, in_specs=in_specs, out_specs=P("aux", both), check_vma=False)
```

```python
import functools

import jax
import jax.numpy as jnp
from jax import lax
from jax.experimental import pallas as pl
from jax.experimental.pallas import tpu as pltpu
from jax.sharding import PartitionSpec as P


NAUX = 1024
AUXG = 8
MU = 512
NU = 64
LAM = 128
SIG = 128
MUC = 128
NGROUPS = 128
UNROLL = 8
HEAD = 8
BF16 = jnp.bfloat16
F32 = jnp.float32
STAGES = ((0, 2, 6, 1, 5), (3, 7, 4))


def fold(low, first, second):
    return (
        jnp.where(low, first, pltpu.roll(second, 64, 1)),
        jnp.where(low, pltpu.roll(first, 64, 1), second),
    )


def half_kernel(dests, count, cost, group, me, x_hbm, occ, *rest):
    outs, (xbuf, turned, sem) = rest[:dests], rest[dests:]
    blocks, slots = cost.shape
    lam_each = LAM // dests
    units = MU // MUC
    first = count[0]
    total = first + count[1]

    def place(i):
        b = jnp.where(i < first, 0, 1)
        return b, i - b * first

    def each_size(i, act):
        b, s = place(i)
        for k in range(1, units + 1):
            @pl.when((cost[b, s] == k) & (i < total))
            def _(k=k):
                act(b, s, i, k)

    def copy(b, s, i, k):
        return pltpu.make_async_copy(
            x_hbm.at[b, s, :, :, pl.ds(0, MUC * k)],
            xbuf.at[i, :, :, pl.ds(0, MUC * k)],
            sem.at[i],
        )

    def fetch(b, s, i, k):
        copy(b, s, i, k).start()
        if k < units:
            xbuf[i, :, :, MUC * k:] = jnp.zeros((AUXG, NU, MU - MUC * k), BF16)

    def issue(i, carry):
        each_size(i, fetch)
        return carry

    lax.fori_loop(0, total, issue, 0)

    shape = (HEAD, 128)
    row = lax.broadcasted_iota(jnp.int32, shape, 0)
    lane = lax.broadcasted_iota(jnp.int32, shape, 1)
    head = jnp.zeros(shape, jnp.int32)
    for b in range(blocks):
        head = jnp.where((row == b) & (lane == slots), count[b], head)
        for s in range(slots):
            head = jnp.where((row == b) & (lane == s), group[b, s], head)
    head = head.astype(F32).astype(BF16)
    for out in outs:
        out[blocks * slots * lam_each:, 0:128] = head
    old = lax.broadcasted_iota(jnp.int32, (LAM, LAM), 0)
    new = lax.broadcasted_iota(jnp.int32, (LAM, LAM), 1)
    moves = old == (me[0] ^ (new // lam_each)) * lam_each + lax.rem(new, lam_each)
    moves = jnp.where(moves, 1.0, 0.0).astype(BF16)
    for b in range(blocks):
        whole = jnp.dot(occ[b], moves, preferred_element_type=F32).astype(BF16)
        for k in range(1, units + 1):
            turned[k - 1, b, 0:MUC * k] = whole[0:MUC * k]
            if k < units:
                turned[k - 1, b, MUC * k:] = jnp.zeros_like(whole[MUC * k:])

    def step(t, carry):
        for u in range(UNROLL):
            each_size(UNROLL * t + u, lambda *which: copy(*which).wait())
        for u in range(UNROLL):
            i = jnp.minimum(UNROLL * t + u, total - 1)
            b, s = place(i)
            x = xbuf[i].reshape(AUXG * NU, MU)
            h = jnp.dot(x, turned[cost[b, s] - 1, b], preferred_element_type=F32)
            ht = h.astype(BF16).T
            at = pl.multiple_of((b * slots + s) * lam_each, lam_each)
            for d in range(dests):
                outs[d][pl.ds(at, lam_each), :] = ht[d * lam_each:(d + 1) * lam_each]
        return carry

    lax.fori_loop(0, (total + UNROLL - 1) // UNROLL, step, 0)


ROWS = NAUX + 32


def response_kernel(sources, last, *rest):
    if last:
        core, rest = rest[0], rest[1:]
    parts, rest = rest[:sources], rest[sources:]
    if last:
        before, columns, keep_ref, send_ref, z, lhs, acc, headint, table, order, ssem, r = rest
    else:
        columns, r, z, lhs, acc, headint, table, order, ssem = rest
    blocks, _, width = columns.shape
    pairs = width // 128
    lam_each = 2 * pairs
    slots = (parts[0].shape[0] - HEAD) // (blocks * lam_each)
    block_rows = 256
    held = block_rows // AUXG

    for s in range(sources):
        rows = parts[s][blocks * slots * lam_each:, 0:128]
        headint[s] = rows.astype(F32).astype(jnp.int32)
    to_scalar = pltpu.make_async_copy(headint, table, ssem.at[0])
    to_scalar.start()
    r[...] = before[...] if last else jnp.zeros_like(r)
    low = lax.broadcasted_iota(jnp.int32, (8, 128), 1) < 64
    to_scalar.wait()
    for b in range(blocks):
        filled = jnp.int32(0)
        for s in range(sources):
            n = table[s, b, slots]

            def spread(ch, carry, s=s, b=b, filled=filled):
                start = pl.multiple_of((b * slots + ch * 4) * lam_each, 4 * lam_each)
                four = parts[s][pl.ds(start, 4 * lam_each), :].astype(F32)
                for i in range(4):
                    at = filled + ch * 4 + i
                    order[at] = table[s, b, ch * 4 + i]
                    for j in range(AUXG // 2):
                        cols = slice(128 * j, 128 * (j + 1))
                        upper = four[i * lam_each:i * lam_each + pairs, cols]
                        lower = four[i * lam_each + pairs:(i + 1) * lam_each, cols]
                        for e, v in enumerate(fold(low, upper, lower)):
                            z[pl.ds(at * AUXG + 2 * j + e, pairs, stride=ROWS), :] = v
                return carry

            lax.fori_loop(0, (n + 3) // 4, spread, 0)
            filled = filled + n

        def multiply(m, carry, b=b, filled=filled):
            for q in range(pairs):
                start = pl.multiple_of(q * ROWS + m * block_rows, 8)
                lhs[:, q * 128:(q + 1) * 128] = z[pl.ds(start, block_rows), :].astype(BF16)
            acc[...] = lax.dot_general(
                lhs[...], columns[b], (((1,), (1,)), ((), ())), preferred_element_type=F32,
            )

            def scatter(i, inner):
                g = order[m * held + i]
                to = pl.ds(pl.multiple_of(g * AUXG, AUXG), AUXG)
                at = pl.ds(pl.multiple_of(i * AUXG, AUXG), AUXG)
                for q in range(r.shape[0]):
                    r[q, to, :] += acc[at, q * 128:(q + 1) * 128]
                return inner

            lax.fori_loop(0, jnp.minimum(held, filled - m * held), scatter, 0)
            return carry

        lax.fori_loop(0, (filled + held - 1) // held, multiply, 0)

    if last:
        is_first = core[0] == 0
        low = lax.broadcasted_iota(jnp.int32, (64, 128), 1) < 64
        for a in range(keep_ref.shape[0]):
            for q in range(keep_ref.shape[1]):
                even, odd = fold(
                    low, r[q, a * 128:a * 128 + 64, :], r[q, a * 128 + 64:a * 128 + 128, :])
                keep_ref[a, q] = jnp.where(is_first, even, odd)
                send_ref[a, q] = jnp.where(is_first, odd, even).astype(BF16)


def local(three_centre, slot_groups, slot_count, block_cost, green_occ, green_vir, target):
    blocks, slots = slot_groups.shape
    dests = lax.axis_size("aux")
    chips = lax.axis_size("chip")
    lam_each = LAM // dests
    pairs = lam_each // 2
    smem = pl.BlockSpec(memory_space=pltpu.SMEM)
    vmem = pl.BlockSpec(memory_space=pltpu.VMEM)
    hbm = pl.BlockSpec(memory_space=pltpu.MemorySpace.HBM)

    held = blocks * slots * lam_each + HEAD
    sent = pl.pallas_call(
        functools.partial(half_kernel, dests),
        out_shape=[jax.ShapeDtypeStruct((held, AUXG * NU), BF16)] * dests,
        in_specs=[smem, smem, smem, smem, hbm, vmem],
        out_specs=[vmem] * dests,
        scratch_shapes=[
            pltpu.VMEM((blocks * slots, AUXG, NU, MU), BF16),
            pltpu.VMEM((MU // MUC, blocks, MU, LAM), BF16),
            pltpu.SemaphoreType.DMA((blocks * slots,)),
        ],
        cost_estimate=pl.CostEstimate(flops=2 * 10**9, bytes_accessed=2 * 10**7, transcendentals=0),
        name="half",
    )(slot_count.reshape(-1), block_cost, slot_groups, lax.axis_index("aux").reshape(1),
      three_centre, green_occ)
    arrived = {0: sent[0]}
    for stage in STAGES:
        for d in stage:
            if d:
                arrived[d] = lax.ppermute(sent[d], "aux", [(i, i ^ d) for i in range(dests)])

    columns = jnp.einsum(
        "qbzit,bnt->bqizn", target.reshape(NAUX, blocks, 2, pairs, SIG), green_vir,
        preferred_element_type=F32,
    ).astype(BF16).reshape(blocks, NAUX, pairs * 128)
    core = lax.axis_index("core").reshape(1)
    running = None
    for number, stage in enumerate(STAGES):
        last = number == len(STAGES) - 1
        inputs = [arrived[d] for d in stage]
        specs = [vmem] * len(stage)
        whole = jax.ShapeDtypeStruct((NAUX // 128, NAUX, 128), F32)
        scratch = [
            pltpu.VMEM((pairs * ROWS, 128), F32),
            pltpu.VMEM((256, pairs * 128), BF16),
            pltpu.VMEM((256, NAUX), F32),
            pltpu.VMEM((len(stage), 8, 128), jnp.int32),
            pltpu.SMEM((len(stage), 8, 128), jnp.int32),
            pltpu.SMEM((NGROUPS + 4,), jnp.int32),
            pltpu.SemaphoreType.DMA((1,)),
        ]
        shape = whole
        if last:
            inputs = [core, *inputs, running]
            specs = [smem, *specs, vmem]
            scratch.append(pltpu.VMEM(whole.shape, F32))
            shape = (
                jax.ShapeDtypeStruct((dests, chips, 64, 128), F32),
                jax.ShapeDtypeStruct((dests, chips, 64, 128), BF16),
            )
        respond = pl.pallas_call(
            functools.partial(response_kernel, len(stage), last),
            out_shape=shape,
            in_specs=[*specs, vmem],
            out_specs=(vmem, vmem) if last else vmem,
            scratch_shapes=scratch,
            compiler_params=pltpu.CompilerParams(vmem_limit_bytes=24 * 2**20),
            cost_estimate=pl.CostEstimate(flops=3 * 10**9, bytes_accessed=10**7, transcendentals=0),
        )
        running = respond(*inputs, columns)
    keep, send = running
    other = lax.ppermute(send, "core", [(0, 1), (1, 0)])
    mine = (keep + other.astype(F32)).astype(BF16).reshape(dests * chips, 64, 128)
    parts = lax.all_to_all(mine, ("aux", "chip"), split_axis=0, concat_axis=0, tiled=True)
    total = jnp.sum(parts.astype(F32), axis=0)
    return jnp.concatenate([total[:, :64], total[:, 64:]], axis=0)


def solution(mesh):
    aux, pair = mesh.devices.shape
    fine = jax.sharding.Mesh(
        mesh.devices.reshape(aux, pair // 2, 2), ("aux", "chip", "core")
    )
    both = ("chip", "core")
    in_specs = (
        P(both, "aux", None, None, None),
        P(both, "aux"),
        P(both, "aux"),
        P(both, "aux"),
        P(both, None, None),
        P(both, None, None),
        P(None, both, "aux", None),
    )

    return jax.shard_map(local, mesh=fine, in_specs=in_specs, out_specs=P("aux", both), check_vma=False)
```

```python
import functools

import jax
import jax.numpy as jnp
from jax import lax
from jax.experimental import pallas as pl
from jax.experimental.pallas import tpu as pltpu
from jax.sharding import PartitionSpec as P


NAUX = 1024
AUXG = 8
MU = 512
NU = 64
LAM = 128
SIG = 128
MUC = 128
NGROUPS = 128
TOGETHER = 4
HEAD = 8
BF16 = jnp.bfloat16
F32 = jnp.float32
STAGES = ((0, 2, 6, 1, 5), (3, 7, 4))


def fold(low, first, second):
    return (
        jnp.where(low, first, pltpu.roll(second, 64, 1)),
        jnp.where(low, pltpu.roll(first, 64, 1), second),
    )


def half_kernel(dests, count, cost, group, me, x_hbm, occ, *rest):
    outs, (xbuf, turned, obuf, headbuf, sem, osem, gsem) = rest[:dests], rest[dests:]
    blocks, slots = cost.shape
    lam_each = LAM // dests
    units = MU // MUC
    chunks = slots // TOGETHER
    tall = TOGETHER * lam_each

    def each_size(b, s, act):
        for k in range(1, units + 1):
            @pl.when((cost[b, s] == k) & (s < count[b]))
            def _(k=k):
                act(b, s, k)

    def copy(b, s, k):
        return pltpu.make_async_copy(
            x_hbm.at[b, s, :, :, pl.ds(0, MUC * k)],
            xbuf.at[b * slots + s, :, :, pl.ds(0, MUC * k)],
            sem.at[b * slots + s],
        )

    def fetch(b, s, k):
        copy(b, s, k).start()
        if k < units:
            xbuf[b * slots + s, :, :, MUC * k:] = jnp.zeros((AUXG, NU, MU - MUC * k), BF16)

    for b in range(blocks):
        def issue(s, carry, b=b):
            each_size(b, s, fetch)
            return carry

        lax.fori_loop(0, count[b], issue, 0)

    shape = (HEAD, 128)
    row = lax.broadcasted_iota(jnp.int32, shape, 0)
    lane = lax.broadcasted_iota(jnp.int32, shape, 1)
    head = jnp.zeros(shape, jnp.int32)
    for b in range(blocks):
        head = jnp.where((row == b) & (lane == slots), count[b], head)
        for s in range(slots):
            head = jnp.where((row == b) & (lane == s), group[b, s], head)
    headbuf[...] = head.astype(F32).astype(BF16)
    end = pl.ds(blocks * slots * lam_each, HEAD)
    heads = [
        pltpu.make_async_copy(headbuf, outs[d].at[end, pl.ds(0, 128)], gsem.at[d])
        for d in range(dests)
    ]
    for one in heads:
        one.start()
    old = lax.broadcasted_iota(jnp.int32, (LAM, LAM), 0)
    new = lax.broadcasted_iota(jnp.int32, (LAM, LAM), 1)
    moves = old == (me[0] ^ (new // lam_each)) * lam_each + lax.rem(new, lam_each)
    moves = jnp.where(moves, 1.0, 0.0).astype(BF16)
    for b in range(blocks):
        turned[b] = jnp.dot(occ[b], moves, preferred_element_type=F32).astype(BF16)

    def out_copy(b, t, d):
        rows = pl.ds(pl.multiple_of((b * chunks + t) * tall, tall), tall)
        return pltpu.make_async_copy(
            obuf.at[d, rows], outs[d].at[rows], osem.at[b * chunks + t, d])

    for b in range(blocks):
        steps = (count[b] + TOGETHER - 1) // TOGETHER

        def step(t, carry, b=b):
            for u in range(TOGETHER):
                each_size(b, TOGETHER * t + u, lambda *which: copy(*which).wait())
            x = xbuf[pl.ds(b * slots + TOGETHER * t, TOGETHER)].reshape(-1, MU)
            h = jnp.dot(x, turned[b], preferred_element_type=F32).astype(BF16)
            for u in range(TOGETHER):
                ht = h[u * AUXG * NU:(u + 1) * AUXG * NU].T
                at = pl.multiple_of((b * slots + TOGETHER * t + u) * lam_each, lam_each)
                for d in range(dests):
                    obuf[d, pl.ds(at, lam_each), :] = ht[d * lam_each:(d + 1) * lam_each]
            for d in range(dests):
                out_copy(b, t, d).start()
            return carry

        lax.fori_loop(0, steps, step, 0)
    for b in range(blocks):
        def finish(t, carry, b=b):
            for d in range(dests):
                out_copy(b, t, d).wait()
            return carry

        lax.fori_loop(0, (count[b] + TOGETHER - 1) // TOGETHER, finish, 0)
    for one in heads:
        one.wait()


ROWS = NAUX + 32


def response_kernel(sources, last, *rest):
    core, rest = rest[0], rest[1:]
    is_first = core[0] == 0
    parts, rest = rest[:sources], rest[sources:]
    if last:
        keep_before, send_before, columns, keep_ref, send_ref = rest[:5]
    else:
        columns, keep_ref, send_ref = rest[:3]
    z, lhs, acc, headint, table, order, ssem, r = rest[-8:]
    blocks, _, width = columns.shape
    pairs = width // 128
    lam_each = 2 * pairs
    slots = (parts[0].shape[0] - HEAD) // (blocks * lam_each)
    block_rows = 256
    held = block_rows // AUXG

    for s in range(sources):
        rows = parts[s][blocks * slots * lam_each:, 0:128]
        headint[s] = rows.astype(F32).astype(jnp.int32)
    to_scalar = pltpu.make_async_copy(headint, table, ssem.at[0])
    to_scalar.start()
    if last:
        keep_ref[...] = keep_before[...]
        r[...] = send_before[...]
    else:
        r[...] = jnp.zeros_like(r)
    low = lax.broadcasted_iota(jnp.int32, (8, 128), 1) < 64
    to_scalar.wait()
    for b in range(blocks):
        filled = jnp.int32(0)
        for s in range(sources):
            n = table[s, b, slots]

            def spread(ch, carry, s=s, b=b, filled=filled):
                start = pl.multiple_of((b * slots + ch * 4) * lam_each, 4 * lam_each)
                four = parts[s][pl.ds(start, 4 * lam_each), :].astype(F32)
                for i in range(4):
                    at = filled + ch * 4 + i
                    order[at] = table[s, b, ch * 4 + i]
                    for j in range(AUXG // 2):
                        cols = slice(128 * j, 128 * (j + 1))
                        upper = four[i * lam_each:i * lam_each + pairs, cols]
                        lower = four[i * lam_each + pairs:(i + 1) * lam_each, cols]
                        for e, v in enumerate(fold(low, upper, lower)):
                            z[pl.ds(at * AUXG + 2 * j + e, pairs, stride=ROWS), :] = v
                return carry

            lax.fori_loop(0, (n + 3) // 4, spread, 0)
            filled = filled + n

        def multiply(m, carry, b=b, filled=filled):
            for q in range(pairs):
                start = pl.multiple_of(q * ROWS + m * block_rows, 8)
                lhs[:, q * 128:(q + 1) * 128] = z[pl.ds(start, block_rows), :].astype(BF16)
            acc[...] = lax.dot_general(
                lhs[...], columns[b], (((1,), (1,)), ((), ())), preferred_element_type=F32,
            )

            def scatter(i, inner):
                g = order[m * held + i]
                at = pl.ds(pl.multiple_of(i * AUXG, AUXG), AUXG)
                if not last:
                    to = pl.ds(pl.multiple_of(g * AUXG, AUXG), AUXG)
                    for q in range(r.shape[0]):
                        r[q, to, :] += acc[at, q * 128:(q + 1) * 128]
                    return inner
                tile, upper = g // 16, lax.rem(g, 16) < 8
                to = pl.ds(pl.multiple_of(lax.rem(g, 8) * AUXG, AUXG), AUXG)
                mask = low == upper
                straight = upper == is_first
                for q in range(r.shape[1]):
                    v = acc[at, q * 128:(q + 1) * 128]
                    w = pltpu.roll(v, 64, 1)
                    keep_ref[tile, q, to, :] += jnp.where(mask, jnp.where(straight, v, w), 0.0)
                    r[tile, q, to, :] += jnp.where(mask, jnp.where(straight, w, v), 0.0)
                return inner

            lax.fori_loop(0, jnp.minimum(held, filled - m * held), scatter, 0)
            return carry

        lax.fori_loop(0, (filled + held - 1) // held, multiply, 0)

    if last:
        send_ref[...] = r[...].astype(BF16)
        return
    low = lax.broadcasted_iota(jnp.int32, (64, 128), 1) < 64
    for a in range(keep_ref.shape[0]):
        for q in range(keep_ref.shape[1]):
            even, odd = fold(low, r[q, a * 128:a * 128 + 64, :], r[q, a * 128 + 64:a * 128 + 128, :])
            keep_ref[a, q] = jnp.where(is_first, even, odd)
            send_ref[a, q] = jnp.where(is_first, odd, even)


def local(three_centre, slot_groups, slot_count, block_cost, green_occ, green_vir, target):
    blocks, slots = slot_groups.shape
    dests = lax.axis_size("aux")
    chips = lax.axis_size("chip")
    lam_each = LAM // dests
    pairs = lam_each // 2
    smem = pl.BlockSpec(memory_space=pltpu.SMEM)
    vmem = pl.BlockSpec(memory_space=pltpu.VMEM)
    hbm = pl.BlockSpec(memory_space=pltpu.MemorySpace.HBM)

    held = blocks * slots * lam_each + HEAD
    sent = pl.pallas_call(
        functools.partial(half_kernel, dests),
        out_shape=[jax.ShapeDtypeStruct((held, AUXG * NU), BF16)] * dests,
        in_specs=[smem, smem, smem, smem, hbm, vmem],
        out_specs=[hbm] * dests,
        scratch_shapes=[
            pltpu.VMEM((blocks * slots, AUXG, NU, MU), BF16),
            pltpu.VMEM((blocks, MU, LAM), BF16),
            pltpu.VMEM((dests, blocks * slots * lam_each, AUXG * NU), BF16),
            pltpu.VMEM((HEAD, 128), BF16),
            pltpu.SemaphoreType.DMA((blocks * slots,)),
            pltpu.SemaphoreType.DMA((blocks * slots // TOGETHER, dests)),
            pltpu.SemaphoreType.DMA((dests,)),
        ],
        cost_estimate=pl.CostEstimate(flops=2 * 10**9, bytes_accessed=2 * 10**7, transcendentals=0),
        name="half",
    )(slot_count.reshape(-1), block_cost, slot_groups, lax.axis_index("aux").reshape(1),
      three_centre, green_occ)
    arrived = {0: sent[0]}
    for stage in STAGES:
        for d in stage:
            if d:
                arrived[d] = lax.ppermute(sent[d], "aux", [(i, i ^ d) for i in range(dests)])

    columns = jnp.einsum(
        "qbzit,bnt->bqizn", target.reshape(NAUX, blocks, 2, pairs, SIG), green_vir,
        preferred_element_type=F32,
    ).astype(BF16).reshape(blocks, NAUX, pairs * 128)
    core = lax.axis_index("core").reshape(1)
    running = None
    for number, stage in enumerate(STAGES):
        last = number == len(STAGES) - 1
        inputs = [arrived[d] for d in stage]
        specs = [vmem] * len(stage)
        scratch = [
            pltpu.VMEM((pairs * ROWS, 128), F32),
            pltpu.VMEM((256, pairs * 128), BF16),
            pltpu.VMEM((256, NAUX), F32),
            pltpu.VMEM((len(stage), 8, 128), jnp.int32),
            pltpu.SMEM((len(stage), 8, 128), jnp.int32),
            pltpu.SMEM((NGROUPS + 4,), jnp.int32),
            pltpu.SemaphoreType.DMA((1,)),
        ]
        folded = (dests, chips, 64, 128)
        shape = (
            jax.ShapeDtypeStruct(folded, F32),
            jax.ShapeDtypeStruct(folded, BF16 if last else F32),
        )
        inputs = [core, *inputs]
        specs = [smem, *specs]
        if last:
            inputs += running
            specs += [vmem, vmem]
        scratch.append(pltpu.VMEM(folded if last else (NAUX // 128, NAUX, 128), F32))
        respond = pl.pallas_call(
            functools.partial(response_kernel, len(stage), last),
            out_shape=shape,
            in_specs=[*specs, vmem],
            out_specs=(vmem, vmem),
            scratch_shapes=scratch,
            compiler_params=pltpu.CompilerParams(vmem_limit_bytes=24 * 2**20),
            cost_estimate=pl.CostEstimate(flops=3 * 10**9, bytes_accessed=10**7, transcendentals=0),
        )
        running = respond(*inputs, columns)
    keep, send = running
    other = lax.ppermute(send, "core", [(0, 1), (1, 0)])
    mine = (keep + other.astype(F32)).astype(BF16).reshape(dests * chips, 64, 128)
    parts = lax.all_to_all(mine, ("aux", "chip"), split_axis=0, concat_axis=0, tiled=True)
    total = jnp.sum(parts.astype(F32), axis=0)
    return jnp.concatenate([total[:, :64], total[:, 64:]], axis=0)


def solution(mesh):
    aux, pair = mesh.devices.shape
    fine = jax.sharding.Mesh(
        mesh.devices.reshape(aux, pair // 2, 2), ("aux", "chip", "core")
    )
    both = ("chip", "core")
    in_specs = (
        P(both, "aux", None, None, None),
        P(both, "aux"),
        P(both, "aux"),
        P(both, "aux"),
        P(both, None, None),
        P(both, None, None),
        P(None, both, "aux", None),
    )

    return jax.shard_map(local, mesh=fine, in_specs=in_specs, out_specs=P("aux", both), check_vma=False)
```

```python
import functools

import jax
import jax.numpy as jnp
from jax import lax
from jax.experimental import pallas as pl
from jax.experimental.pallas import tpu as pltpu
from jax.sharding import PartitionSpec as P


NAUX = 1024
AUXG = 8
MU = 512
NU = 64
LAM = 128
SIG = 128
MUC = 128
NGROUPS = 128
TOGETHER = 4
HEAD = 8
BF16 = jnp.bfloat16
F32 = jnp.float32
STAGES = ((0, 2, 6, 1, 5), (3,), (7, 4))


def fold(low, first, second):
    return (
        jnp.where(low, first, pltpu.roll(second, 64, 1)),
        jnp.where(low, pltpu.roll(first, 64, 1), second),
    )


def half_kernel(dests, count, cost, group, me, x_hbm, occ, *rest):
    outs, (xbuf, turned, obuf, headbuf, sem, osem, gsem) = rest[:dests], rest[dests:]
    blocks, slots = cost.shape
    lam_each = LAM // dests
    units = MU // MUC
    chunks = slots // TOGETHER
    tall = TOGETHER * lam_each

    def each_size(b, s, act):
        for k in range(1, units + 1):
            @pl.when((cost[b, s] == k) & (s < count[b]))
            def _(k=k):
                act(b, s, k)

    def copy(b, s, k):
        return pltpu.make_async_copy(
            x_hbm.at[b, s, :, :, pl.ds(0, MUC * k)],
            xbuf.at[b * slots + s, :, :, pl.ds(0, MUC * k)],
            sem.at[b * slots + s],
        )

    def fetch(b, s, k):
        copy(b, s, k).start()
        if k < units:
            xbuf[b * slots + s, :, :, MUC * k:] = jnp.zeros((AUXG, NU, MU - MUC * k), BF16)

    for b in range(blocks):
        def issue(s, carry, b=b):
            each_size(b, s, fetch)
            return carry

        lax.fori_loop(0, count[b], issue, 0)

    shape = (HEAD, 128)
    row = lax.broadcasted_iota(jnp.int32, shape, 0)
    lane = lax.broadcasted_iota(jnp.int32, shape, 1)
    head = jnp.zeros(shape, jnp.int32)
    for b in range(blocks):
        head = jnp.where((row == b) & (lane == slots), count[b], head)
        for s in range(slots):
            head = jnp.where((row == b) & (lane == s), group[b, s], head)
    headbuf[...] = head.astype(F32).astype(BF16)
    end = pl.ds(blocks * slots * lam_each, HEAD)
    heads = [
        pltpu.make_async_copy(headbuf, outs[d].at[end, pl.ds(0, 128)], gsem.at[d])
        for d in range(dests)
    ]
    for one in heads:
        one.start()
    old = lax.broadcasted_iota(jnp.int32, (LAM, LAM), 0)
    new = lax.broadcasted_iota(jnp.int32, (LAM, LAM), 1)
    moves = old == (me[0] ^ (new // lam_each)) * lam_each + lax.rem(new, lam_each)
    moves = jnp.where(moves, 1.0, 0.0).astype(BF16)
    for b in range(blocks):
        turned[b] = jnp.dot(occ[b], moves, preferred_element_type=F32).astype(BF16)

    def out_copy(b, t, d):
        rows = pl.ds(pl.multiple_of((b * chunks + t) * tall, tall), tall)
        return pltpu.make_async_copy(
            obuf.at[d, rows], outs[d].at[rows], osem.at[b * chunks + t, d])

    for b in range(blocks):
        steps = (count[b] + TOGETHER - 1) // TOGETHER

        def step(t, carry, b=b):
            for u in range(TOGETHER):
                each_size(b, TOGETHER * t + u, lambda *which: copy(*which).wait())
            x = xbuf[pl.ds(b * slots + TOGETHER * t, TOGETHER)].reshape(-1, MU)
            h = jnp.dot(x, turned[b], preferred_element_type=F32).astype(BF16)
            for u in range(TOGETHER):
                ht = h[u * AUXG * NU:(u + 1) * AUXG * NU].T
                at = pl.multiple_of((b * slots + TOGETHER * t + u) * lam_each, lam_each)
                for d in range(dests):
                    obuf[d, pl.ds(at, lam_each), :] = ht[d * lam_each:(d + 1) * lam_each]
            for d in range(dests):
                out_copy(b, t, d).start()
            return carry

        lax.fori_loop(0, steps, step, 0)
    for b in range(blocks):
        def finish(t, carry, b=b):
            for d in range(dests):
                out_copy(b, t, d).wait()
            return carry

        lax.fori_loop(0, (count[b] + TOGETHER - 1) // TOGETHER, finish, 0)
    for one in heads:
        one.wait()


ROWS = NAUX + 32


def response_kernel(sources, begun, last, *rest):
    if last:
        core, rest = rest[0], rest[1:]
    parts, rest = rest[:sources], rest[sources:]
    if last:
        before, columns, keep_ref, send_ref, z, lhs, acc, headint, table, order, ssem, r = rest
    elif begun:
        before, columns, r, z, lhs, acc, headint, table, order, ssem = rest
    else:
        columns, r, z, lhs, acc, headint, table, order, ssem = rest
    blocks, _, width = columns.shape
    pairs = width // 128
    lam_each = 2 * pairs
    slots = (parts[0].shape[0] - HEAD) // (blocks * lam_each)
    block_rows = 256
    held = block_rows // AUXG

    for s in range(sources):
        rows = parts[s][blocks * slots * lam_each:, 0:128]
        headint[s] = rows.astype(F32).astype(jnp.int32)
    to_scalar = pltpu.make_async_copy(headint, table, ssem.at[0])
    to_scalar.start()
    r[...] = before[...] if begun else jnp.zeros_like(r)
    low = lax.broadcasted_iota(jnp.int32, (8, 128), 1) < 64
    to_scalar.wait()
    for b in range(blocks):
        filled = jnp.int32(0)
        for s in range(sources):
            n = table[s, b, slots]

            def spread(ch, carry, s=s, b=b, filled=filled):
                start = pl.multiple_of((b * slots + ch * 4) * lam_each, 4 * lam_each)
                four = parts[s][pl.ds(start, 4 * lam_each), :].astype(F32)
                for i in range(4):
                    at = filled + ch * 4 + i
                    order[at] = table[s, b, ch * 4 + i]
                    for j in range(AUXG // 2):
                        cols = slice(128 * j, 128 * (j + 1))
                        upper = four[i * lam_each:i * lam_each + pairs, cols]
                        lower = four[i * lam_each + pairs:(i + 1) * lam_each, cols]
                        for e, v in enumerate(fold(low, upper, lower)):
                            z[pl.ds(at * AUXG + 2 * j + e, pairs, stride=ROWS), :] = v
                return carry

            lax.fori_loop(0, (n + 3) // 4, spread, 0)
            filled = filled + n

        def multiply(m, carry, b=b, filled=filled):
            for q in range(pairs):
                start = pl.multiple_of(q * ROWS + m * block_rows, 8)
                lhs[:, q * 128:(q + 1) * 128] = z[pl.ds(start, block_rows), :].astype(BF16)
            acc[...] = lax.dot_general(
                lhs[...], columns[b], (((1,), (1,)), ((), ())), preferred_element_type=F32,
            )

            here = jnp.minimum(held, filled - m * held)

            def scatter(t, inner):
                places, sums = [], []
                for u in range(4):
                    i = t * 4 + u
                    g = jnp.where(i < here, order[m * held + i], NGROUPS)
                    to = pl.ds(pl.multiple_of(g * AUXG, AUXG), AUXG)
                    at = pl.ds(pl.multiple_of(i * AUXG, AUXG), AUXG)
                    places.append(to)
                    sums.append([
                        r[q, to, :] + acc[at, q * 128:(q + 1) * 128] for q in range(r.shape[0])
                    ])
                for to, sum_here in zip(places, sums):
                    for q in range(r.shape[0]):
                        r[q, to, :] = sum_here[q]
                return inner

            lax.fori_loop(0, (here + 3) // 4, scatter, 0)
            return carry

        lax.fori_loop(0, (filled + held - 1) // held, multiply, 0)

    if last:
        is_first = core[0] == 0
        low = lax.broadcasted_iota(jnp.int32, (64, 128), 1) < 64
        for a in range(keep_ref.shape[0]):
            for q in range(keep_ref.shape[1]):
                even, odd = fold(
                    low, r[q, a * 128:a * 128 + 64, :], r[q, a * 128 + 64:a * 128 + 128, :])
                keep_ref[a, q] = jnp.where(is_first, even, odd)
                send_ref[a, q] = jnp.where(is_first, odd, even).astype(BF16)


def local(three_centre, slot_groups, slot_count, block_cost, green_occ, green_vir, target):
    blocks, slots = slot_groups.shape
    dests = lax.axis_size("aux")
    chips = lax.axis_size("chip")
    lam_each = LAM // dests
    pairs = lam_each // 2
    smem = pl.BlockSpec(memory_space=pltpu.SMEM)
    vmem = pl.BlockSpec(memory_space=pltpu.VMEM)
    hbm = pl.BlockSpec(memory_space=pltpu.MemorySpace.HBM)

    held = blocks * slots * lam_each + HEAD
    sent = pl.pallas_call(
        functools.partial(half_kernel, dests),
        out_shape=[jax.ShapeDtypeStruct((held, AUXG * NU), BF16)] * dests,
        in_specs=[smem, smem, smem, smem, hbm, vmem],
        out_specs=[hbm] * dests,
        scratch_shapes=[
            pltpu.VMEM((blocks * slots, AUXG, NU, MU), BF16),
            pltpu.VMEM((blocks, MU, LAM), BF16),
            pltpu.VMEM((dests, blocks * slots * lam_each, AUXG * NU), BF16),
            pltpu.VMEM((HEAD, 128), BF16),
            pltpu.SemaphoreType.DMA((blocks * slots,)),
            pltpu.SemaphoreType.DMA((blocks * slots // TOGETHER, dests)),
            pltpu.SemaphoreType.DMA((dests,)),
        ],
        cost_estimate=pl.CostEstimate(flops=2 * 10**9, bytes_accessed=2 * 10**7, transcendentals=0),
        name="half",
    )(slot_count.reshape(-1), block_cost, slot_groups, lax.axis_index("aux").reshape(1),
      three_centre, green_occ)
    arrived = {0: sent[0]}
    for stage in STAGES:
        for d in stage:
            if d:
                arrived[d] = lax.ppermute(sent[d], "aux", [(i, i ^ d) for i in range(dests)])

    columns = jnp.einsum(
        "qbzit,bnt->bqizn", target.reshape(NAUX, blocks, 2, pairs, SIG), green_vir,
        preferred_element_type=F32,
    ).astype(BF16).reshape(blocks, NAUX, pairs * 128)
    core = lax.axis_index("core").reshape(1)
    running = None
    for number, stage in enumerate(STAGES):
        last = number == len(STAGES) - 1
        inputs = [arrived[d] for d in stage]
        specs = [vmem] * len(stage)
        whole = jax.ShapeDtypeStruct((NAUX // 128, NAUX + AUXG, 128), F32)
        scratch = [
            pltpu.VMEM((pairs * ROWS, 128), F32),
            pltpu.VMEM((256, pairs * 128), BF16),
            pltpu.VMEM((256, NAUX), F32),
            pltpu.VMEM((len(stage), 8, 128), jnp.int32),
            pltpu.SMEM((len(stage), 8, 128), jnp.int32),
            pltpu.SMEM((NGROUPS + 4,), jnp.int32),
            pltpu.SemaphoreType.DMA((1,)),
        ]
        shape = whole
        if number:
            inputs.append(running)
            specs.append(vmem)
        if last:
            inputs = [core, *inputs]
            specs = [smem, *specs]
            scratch.append(pltpu.VMEM(whole.shape, F32))
            shape = (
                jax.ShapeDtypeStruct((dests, chips, 64, 128), F32),
                jax.ShapeDtypeStruct((dests, chips, 64, 128), BF16),
            )
        respond = pl.pallas_call(
            functools.partial(response_kernel, len(stage), number > 0, last),
            out_shape=shape,
            in_specs=[*specs, vmem],
            out_specs=(vmem, vmem) if last else vmem,
            scratch_shapes=scratch,
            compiler_params=pltpu.CompilerParams(vmem_limit_bytes=24 * 2**20),
            cost_estimate=pl.CostEstimate(flops=3 * 10**9, bytes_accessed=10**7, transcendentals=0),
        )
        running = respond(*inputs, columns)
    keep, send = running
    other = lax.ppermute(send, "core", [(0, 1), (1, 0)])
    mine = (keep + other.astype(F32)).astype(BF16).reshape(dests * chips, 64, 128)
    parts = lax.all_to_all(mine, ("aux", "chip"), split_axis=0, concat_axis=0, tiled=True)
    total = jnp.sum(parts.astype(F32), axis=0)
    return jnp.concatenate([total[:, :64], total[:, 64:]], axis=0)


def solution(mesh):
    aux, pair = mesh.devices.shape
    fine = jax.sharding.Mesh(
        mesh.devices.reshape(aux, pair // 2, 2), ("aux", "chip", "core")
    )
    both = ("chip", "core")
    in_specs = (
        P(both, "aux", None, None, None),
        P(both, "aux"),
        P(both, "aux"),
        P(both, "aux"),
        P(both, None, None),
        P(both, None, None),
        P(None, both, "aux", None),
    )

    return jax.shard_map(local, mesh=fine, in_specs=in_specs, out_specs=P("aux", both), check_vma=False)
```

```python
import functools

import jax
import jax.numpy as jnp
from jax import lax
from jax.experimental import pallas as pl
from jax.experimental.pallas import tpu as pltpu
from jax.sharding import PartitionSpec as P


NAUX = 1024
AUXG = 8
MU = 512
NU = 64
LAM = 128
SIG = 128
MUC = 128
NGROUPS = 128
TOGETHER = 4
HEAD = 8
BF16 = jnp.bfloat16
F32 = jnp.float32
STAGES = ((0, 2, 6, 4), (5, 3), (1, 7))
ISSUE = (5, 2, 3, 6, 7, 4, 1)


def fold(low, first, second):
    return (
        jnp.where(low, first, pltpu.roll(second, 64, 1)),
        jnp.where(low, pltpu.roll(first, 64, 1), second),
    )


def half_kernel(dests, count, cost, group, me, x_hbm, occ, *rest):
    outs, (xbuf, turned, obuf, headbuf, sem, osem, gsem) = rest[:dests], rest[dests:]
    blocks, slots = cost.shape
    lam_each = LAM // dests
    units = MU // MUC
    chunks = slots // TOGETHER
    tall = TOGETHER * lam_each

    def each_size(b, s, act):
        for k in range(1, units + 1):
            @pl.when((cost[b, s] == k) & (s < count[b]))
            def _(k=k):
                act(b, s, k)

    def copy(b, s, k):
        return pltpu.make_async_copy(
            x_hbm.at[b, s, :, :, pl.ds(0, MUC * k)],
            xbuf.at[b * slots + s, :, :, pl.ds(0, MUC * k)],
            sem.at[b * slots + s],
        )

    def fetch(b, s, k):
        copy(b, s, k).start()
        if k < units:
            xbuf[b * slots + s, :, :, MUC * k:] = jnp.zeros((AUXG, NU, MU - MUC * k), BF16)

    for b in range(blocks):
        def issue(s, carry, b=b):
            each_size(b, s, fetch)
            return carry

        lax.fori_loop(0, count[b], issue, 0)

    shape = (HEAD, 128)
    row = lax.broadcasted_iota(jnp.int32, shape, 0)
    lane = lax.broadcasted_iota(jnp.int32, shape, 1)
    head = jnp.zeros(shape, jnp.int32)
    for b in range(blocks):
        head = jnp.where((row == b) & (lane == slots), count[b], head)
        for s in range(slots):
            head = jnp.where((row == b) & (lane == s), group[b, s], head)
    headbuf[...] = head.astype(F32).astype(BF16)
    end = pl.ds(blocks * slots * lam_each, HEAD)
    heads = [
        pltpu.make_async_copy(headbuf, outs[d].at[end, pl.ds(0, 128)], gsem.at[d])
        for d in range(dests)
    ]
    for one in heads:
        one.start()
    old = lax.broadcasted_iota(jnp.int32, (LAM, LAM), 0)
    new = lax.broadcasted_iota(jnp.int32, (LAM, LAM), 1)
    moves = old == (me[0] ^ (new // lam_each)) * lam_each + lax.rem(new, lam_each)
    moves = jnp.where(moves, 1.0, 0.0).astype(BF16)
    for b in range(blocks):
        turned[b] = jnp.dot(occ[b], moves, preferred_element_type=F32).astype(BF16)

    def out_copy(b, t, d):
        rows = pl.ds(pl.multiple_of((b * chunks + t) * tall, tall), tall)
        return pltpu.make_async_copy(
            obuf.at[d, rows], outs[d].at[rows], osem.at[b * chunks + t, d])

    for b in range(blocks):
        steps = (count[b] + TOGETHER - 1) // TOGETHER

        def step(t, carry, b=b):
            for u in range(TOGETHER):
                each_size(b, TOGETHER * t + u, lambda *which: copy(*which).wait())
            x = xbuf[pl.ds(b * slots + TOGETHER * t, TOGETHER)].reshape(-1, MU)
            h = jnp.dot(x, turned[b], preferred_element_type=F32).astype(BF16)
            for u in range(TOGETHER):
                ht = h[u * AUXG * NU:(u + 1) * AUXG * NU].T
                at = pl.multiple_of((b * slots + TOGETHER * t + u) * lam_each, lam_each)
                for d in range(dests):
                    obuf[d, pl.ds(at, lam_each), :] = ht[d * lam_each:(d + 1) * lam_each]
            for d in range(dests):
                out_copy(b, t, d).start()
            return carry

        lax.fori_loop(0, steps, step, 0)
    for b in range(blocks):
        def finish(t, carry, b=b):
            for d in range(dests):
                out_copy(b, t, d).wait()
            return carry

        lax.fori_loop(0, (count[b] + TOGETHER - 1) // TOGETHER, finish, 0)
    for one in heads:
        one.wait()


ROWS = NAUX + 32


def response_kernel(sources, begun, last, *rest):
    if last:
        core, rest = rest[0], rest[1:]
    parts, rest = rest[:sources], rest[sources:]
    if last:
        before, columns, keep_ref, send_ref, z, lhs, acc, headint, table, order, ssem, r = rest
    elif begun:
        before, columns, r, z, lhs, acc, headint, table, order, ssem = rest
    else:
        columns, r, z, lhs, acc, headint, table, order, ssem = rest
    blocks, _, width = columns.shape
    pairs = width // 128
    lam_each = 2 * pairs
    slots = (parts[0].shape[0] - HEAD) // (blocks * lam_each)
    block_rows = 256
    held = block_rows // AUXG

    for s in range(sources):
        rows = parts[s][blocks * slots * lam_each:, 0:128]
        headint[s] = rows.astype(F32).astype(jnp.int32)
    to_scalar = pltpu.make_async_copy(headint, table, ssem.at[0])
    to_scalar.start()
    r[...] = before[...] if begun else jnp.zeros_like(r)
    low = lax.broadcasted_iota(jnp.int32, (8, 128), 1) < 64
    to_scalar.wait()
    for b in range(blocks):
        filled = jnp.int32(0)
        for s in range(sources):
            n = table[s, b, slots]

            def spread(ch, carry, s=s, b=b, filled=filled):
                start = pl.multiple_of((b * slots + ch * 4) * lam_each, 4 * lam_each)
                four = parts[s][pl.ds(start, 4 * lam_each), :].astype(F32)
                for i in range(4):
                    at = filled + ch * 4 + i
                    order[at] = table[s, b, ch * 4 + i]
                    for j in range(AUXG // 2):
                        cols = slice(128 * j, 128 * (j + 1))
                        upper = four[i * lam_each:i * lam_each + pairs, cols]
                        lower = four[i * lam_each + pairs:(i + 1) * lam_each, cols]
                        for e, v in enumerate(fold(low, upper, lower)):
                            z[pl.ds(at * AUXG + 2 * j + e, pairs, stride=ROWS), :] = v
                return carry

            lax.fori_loop(0, (n + 3) // 4, spread, 0)
            filled = filled + n

        def multiply(m, carry, b=b, filled=filled):
            for q in range(pairs):
                start = pl.multiple_of(q * ROWS + m * block_rows, 8)
                lhs[:, q * 128:(q + 1) * 128] = z[pl.ds(start, block_rows), :].astype(BF16)
            acc[...] = lax.dot_general(
                lhs[...], columns[b], (((1,), (1,)), ((), ())), preferred_element_type=F32,
            )

            here = jnp.minimum(held, filled - m * held)

            def scatter(t, inner):
                places, sums = [], []
                for u in range(4):
                    i = t * 4 + u
                    g = jnp.where(i < here, order[m * held + i], NGROUPS)
                    to = pl.ds(pl.multiple_of(g * AUXG, AUXG), AUXG)
                    at = pl.ds(pl.multiple_of(i * AUXG, AUXG), AUXG)
                    places.append(to)
                    sums.append([
                        r[q, to, :] + acc[at, q * 128:(q + 1) * 128] for q in range(r.shape[0])
                    ])
                for to, sum_here in zip(places, sums):
                    for q in range(r.shape[0]):
                        r[q, to, :] = sum_here[q]
                return inner

            lax.fori_loop(0, (here + 3) // 4, scatter, 0)
            return carry

        lax.fori_loop(0, (filled + held - 1) // held, multiply, 0)

    if last:
        is_first = core[0] == 0
        low = lax.broadcasted_iota(jnp.int32, (64, 128), 1) < 64
        for a in range(keep_ref.shape[0]):
            for q in range(keep_ref.shape[1]):
                even, odd = fold(
                    low, r[q, a * 128:a * 128 + 64, :], r[q, a * 128 + 64:a * 128 + 128, :])
                keep_ref[a, q] = jnp.where(is_first, even, odd)
                send_ref[a, q] = jnp.where(is_first, odd, even).astype(BF16)


def local(three_centre, slot_groups, slot_count, block_cost, green_occ, green_vir, target):
    blocks, slots = slot_groups.shape
    dests = lax.axis_size("aux")
    chips = lax.axis_size("chip")
    lam_each = LAM // dests
    pairs = lam_each // 2
    smem = pl.BlockSpec(memory_space=pltpu.SMEM)
    vmem = pl.BlockSpec(memory_space=pltpu.VMEM)
    hbm = pl.BlockSpec(memory_space=pltpu.MemorySpace.HBM)

    held = blocks * slots * lam_each + HEAD
    sent = pl.pallas_call(
        functools.partial(half_kernel, dests),
        out_shape=[jax.ShapeDtypeStruct((held, AUXG * NU), BF16)] * dests,
        in_specs=[smem, smem, smem, smem, hbm, vmem],
        out_specs=[hbm] * dests,
        scratch_shapes=[
            pltpu.VMEM((blocks * slots, AUXG, NU, MU), BF16),
            pltpu.VMEM((blocks, MU, LAM), BF16),
            pltpu.VMEM((dests, blocks * slots * lam_each, AUXG * NU), BF16),
            pltpu.VMEM((HEAD, 128), BF16),
            pltpu.SemaphoreType.DMA((blocks * slots,)),
            pltpu.SemaphoreType.DMA((blocks * slots // TOGETHER, dests)),
            pltpu.SemaphoreType.DMA((dests,)),
        ],
        cost_estimate=pl.CostEstimate(flops=2 * 10**9, bytes_accessed=2 * 10**7, transcendentals=0),
        name="half",
    )(slot_count.reshape(-1), block_cost, slot_groups, lax.axis_index("aux").reshape(1),
      three_centre, green_occ)

    def swap(value, d):
        return lax.ppermute(value, "aux", [(i, i ^ d) for i in range(dests)])

    arrived = {0: sent[0]}
    for d in ISSUE:
        arrived[d] = swap(sent[d], 1 if d % 2 else d)
    for d in ISSUE:
        if d % 2 and d > 1:
            arrived[d] = swap(arrived[d], d - 1)

    columns = jnp.einsum(
        "qbzit,bnt->bqizn", target.reshape(NAUX, blocks, 2, pairs, SIG), green_vir,
        preferred_element_type=F32,
    ).astype(BF16).reshape(blocks, NAUX, pairs * 128)
    core = lax.axis_index("core").reshape(1)
    running = None
    for number, stage in enumerate(STAGES):
        last = number == len(STAGES) - 1
        inputs = [arrived[d] for d in stage]
        specs = [vmem] * len(stage)
        whole = jax.ShapeDtypeStruct((NAUX // 128, NAUX + AUXG, 128), F32)
        scratch = [
            pltpu.VMEM((pairs * ROWS, 128), F32),
            pltpu.VMEM((256, pairs * 128), BF16),
            pltpu.VMEM((256, NAUX), F32),
            pltpu.VMEM((len(stage), 8, 128), jnp.int32),
            pltpu.SMEM((len(stage), 8, 128), jnp.int32),
            pltpu.SMEM((NGROUPS + 4,), jnp.int32),
            pltpu.SemaphoreType.DMA((1,)),
        ]
        shape = whole
        if number:
            inputs.append(running)
            specs.append(vmem)
        if last:
            inputs = [core, *inputs]
            specs = [smem, *specs]
            scratch.append(pltpu.VMEM(whole.shape, F32))
            shape = (
                jax.ShapeDtypeStruct((dests, chips, 64, 128), F32),
                jax.ShapeDtypeStruct((dests, chips, 64, 128), BF16),
            )
        respond = pl.pallas_call(
            functools.partial(response_kernel, len(stage), number > 0, last),
            out_shape=shape,
            in_specs=[*specs, vmem],
            out_specs=(vmem, vmem) if last else vmem,
            scratch_shapes=scratch,
            compiler_params=pltpu.CompilerParams(vmem_limit_bytes=24 * 2**20),
            cost_estimate=pl.CostEstimate(flops=3 * 10**9, bytes_accessed=10**7, transcendentals=0),
        )
        running = respond(*inputs, columns)
    keep, send = running
    other = lax.ppermute(send, "core", [(0, 1), (1, 0)])
    mine = (keep + other.astype(F32)).astype(BF16).reshape(dests * chips, 64, 128)
    parts = lax.all_to_all(mine, ("aux", "chip"), split_axis=0, concat_axis=0, tiled=True)
    total = jnp.sum(parts.astype(F32), axis=0)
    return jnp.concatenate([total[:, :64], total[:, 64:]], axis=0)


def solution(mesh):
    aux, pair = mesh.devices.shape
    fine = jax.sharding.Mesh(
        mesh.devices.reshape(aux, pair // 2, 2), ("aux", "chip", "core")
    )
    both = ("chip", "core")
    in_specs = (
        P(both, "aux", None, None, None),
        P(both, "aux"),
        P(both, "aux"),
        P(both, "aux"),
        P(both, None, None),
        P(both, None, None),
        P(None, both, "aux", None),
    )

    return jax.shard_map(local, mesh=fine, in_specs=in_specs, out_specs=P("aux", both), check_vma=False)
```
